32 devices in a mesh: dom: 8 (over z, y), sub: 4 (over x, core).
Axes of the slice: x: 2, y: 2, z: 4, core: 2. Of those that a mesh axis runs over, the one named last changes fastest.
Arguments:
- fine_latent: bfloat16 [1024, 64, 128], P(('dom', 'sub')), may hold values from -6 to 6
- coarse_latent: bfloat16 [256, 64, 128], P(('dom', 'sub')), may hold values from -6 to 6
- adj_index: int32 [1024, 16], P(('dom', 'sub')), may hold values from 0 to 63
- adj_weight: bfloat16 [1024, 64, 1024], P(('dom', 'sub')), may hold values from -0.1875 to 0.1875
- interp_slot: int32 [1024, 4], P(('dom', 'sub')), may hold values from 0 to 31
- interp_weight: bfloat16 [1024, 64, 256], P(('dom', 'sub')), may hold values from -0.375 to 0.375
- coarse_send: int32 [32, 32, 1], P(('dom', 'sub')), may hold values from 0 to 7
- halo_sub_send: int32 [32, 4, 4], P(('dom', 'sub')), may hold values from 0 to 31
- halo_dom_send: int32 [32, 2, 8], P(('dom', 'sub')), may hold values from 0 to 31
- block_count: int32 [32], P(('dom', 'sub')), may hold values from 16 to 32, as said below
- w_in: bfloat16 [2, 384, 128], replicated, may hold values from -0.3125 to 0.3125
- b_in: float32 [2, 128], replicated, may hold values from -3 to 3
- w_out: bfloat16 [2, 128, 128], replicated, may hold values from -0.5 to 0.5
- ln_gain: float32 [2, 128], replicated, may hold values from 0.25 to 1.75
Outputs:
- fine_out: bfloat16 [1024, 64, 128], P(('dom', 'sub'))
The draws below stay inside these ranges and needn't reach their ends.
Inputs may be any that keep to these rules, and one draw needn't show every extreme that they name: `block_count`: some device has all 32 blocks live and some has half of them.
All inputs are finite; a program needn't handle non-finite values.
Results may differ from the reference program's by a relative error of at most 0.0058.
Values may be sent and summed in bfloat16 or wider, within the bound.
A program may use at most 64 MiB of HBM per device.

```python
import jax
import jax.numpy as jnp
from jax import lax

BLK = 64
LAT = 128
FBLK_DEV = 32
CBLK_DEV = 8
K_A = 16
K_I = 4
SLOTS = 1
HS = 4
HD = 8
STEPS = 2
SHARDS = 32
POOL = 64
FINE_BLKS = 1024
COARSE_BLKS = 256
N_DOM = 8
N_SUB = 4


def draw_block_count(key, part):
    lowest = FBLK_DEV // 2
    counts = jax.random.randint(key, (SHARDS,), lowest, FBLK_DEV + 1)
    order = jax.random.permutation(jax.random.fold_in(key, 7), SHARDS)
    counts = counts.at[order[0]].set(FBLK_DEV).at[order[1]].set(lowest)
    return counts.astype(jnp.int32)


def plant(entries, key, smallest, largest):
    shape = entries.shape
    place = [jax.random.randint(jax.random.fold_in(key, axis), (), 0, shape[axis]) for axis in range(len(shape))]
    entries = entries.at[tuple(place)].set(smallest)
    longest = shape.index(max(shape))
    place[longest] = (place[longest] + 1) % shape[longest]
    return entries.at[tuple(place)].set(largest)


def block_scale(stream_key, shape, cuts, least, high):
    def one(dim, shards_of):
        draws = jax.random.uniform(jax.random.fold_in(jax.random.fold_in(stream_key, 6), dim), (shards_of,), jnp.float32, least / len(cuts), high / len(cuts))
        return jnp.repeat(jnp.exp(draws), shape[dim] // shards_of).reshape((-1,) + (1,) * (len(shape) - dim - 1))

    loudness = one(*cuts[0])
    for cut in cuts[1:]:
        loudness = loudness * one(*cut)
    return loudness


def scatter_about(key, dims, width, bound, pieces=(), kind=jnp.bfloat16):
    drawn = width * jax.random.normal(key, dims, jnp.float32)
    if pieces:
        drawn = drawn * block_scale(key, dims, pieces, -0.22, 0.18)
    return jnp.clip(drawn, -bound, bound).astype(kind)


def setup_inputs(seed: int = 0) -> dict:
    key_of = jax.random.split(jax.random.key(seed), 15)
    fine_latent = scatter_about(key_of[0], (FINE_BLKS, BLK, LAT), 1.0, 6.0, ((0, 32),))
    coarse_latent = scatter_about(key_of[1], (COARSE_BLKS, BLK, LAT), 1.0, 6.0, ((0, 32),))
    adj_index = plant(jax.random.randint(key_of[2], (FINE_BLKS, K_A), 0, POOL), jax.random.fold_in(key_of[2], 1), 0, POOL - 1).astype(jnp.int32)
    adj_weight = scatter_about(key_of[3], (FINE_BLKS, BLK, K_A * BLK), (K_A * BLK) ** -0.5, 0.1875, ((0, 32),))
    interp_slot = plant(jax.random.randint(key_of[4], (FINE_BLKS, K_I), 0, SHARDS * SLOTS), jax.random.fold_in(key_of[4], 1), 0, (SHARDS * SLOTS) - 1).astype(jnp.int32)
    interp_weight = scatter_about(key_of[5], (FINE_BLKS, BLK, K_I * BLK), (K_I * BLK) ** -0.5, 0.375, ((0, 32),))
    coarse_send = plant(jax.random.randint(key_of[6], (SHARDS, SHARDS, SLOTS), 0, CBLK_DEV), jax.random.fold_in(key_of[6], 1), 0, CBLK_DEV - 1).astype(jnp.int32)
    halo_sub_send = plant(jax.random.randint(key_of[7], (SHARDS, N_SUB, HS), 0, FBLK_DEV), jax.random.fold_in(key_of[7], 1), 0, FBLK_DEV - 1).astype(jnp.int32)
    halo_dom_send = plant(jax.random.randint(key_of[8], (SHARDS, 2, HD), 0, FBLK_DEV), jax.random.fold_in(key_of[8], 1), 0, FBLK_DEV - 1).astype(jnp.int32)
    block_count = draw_block_count(jax.random.fold_in(key_of[14], 71), 0)
    w_in = scatter_about(key_of[10], (STEPS, 3 * LAT, LAT), (3 * LAT) ** -0.5, 0.3125)
    b_in = scatter_about(key_of[11], (STEPS, LAT), 0.5, 3.0, (), jnp.float32)
    w_out = scatter_about(key_of[12], (STEPS, LAT, LAT), LAT ** -0.5, 0.5)
    ln_gain = jnp.clip(1.0 + 0.15 * jax.random.normal(key_of[13], (STEPS, LAT), jnp.float32), 0.25, 1.75)
    return dict(fine_latent=fine_latent, coarse_latent=coarse_latent, adj_index=adj_index, adj_weight=adj_weight, interp_slot=interp_slot, interp_weight=interp_weight, coarse_send=coarse_send, halo_sub_send=halo_sub_send, halo_dom_send=halo_dom_send, block_count=block_count, w_in=w_in, b_in=b_in, w_out=w_out, ln_gain=ln_gain)


def layer_norm(values, ln_scale):
    average = lax.optimization_barrier(jnp.mean(values, axis=-1, keepdims=True))
    centred = values - average
    variance = lax.optimization_barrier(jnp.mean(centred * centred, axis=-1, keepdims=True))
    return centred * lax.rsqrt(variance + 1e-05) * ln_scale

def node_update(latent, summed, interp, w_first, b_first, w_second, ln_scale, live_mask):
    joined = jnp.concatenate([latent, summed, interp], axis=-1)
    hidden = jnp.einsum('bic,cl->bil', joined.astype(jnp.float32), w_first.astype(jnp.float32)) + b_first
    hidden = jax.nn.relu(hidden).astype(jnp.bfloat16)
    output = jnp.einsum('bic,cl->bil', hidden.astype(jnp.float32), w_second.astype(jnp.float32))
    updated = latent.astype(jnp.float32) + layer_norm(output, ln_scale)
    return jnp.where(live_mask[:, None, None], updated, jnp.zeros_like(updated)).astype(jnp.bfloat16)

def reference(fine_latent, coarse_latent, adj_index, adj_weight, interp_slot, interp_weight, coarse_send, halo_sub_send, halo_dom_send, block_count, w_in, b_in, w_out, ln_gain):
    fine = fine_latent.reshape(SHARDS, FBLK_DEV, BLK, LAT)
    adj_ids = adj_index.reshape(SHARDS, FBLK_DEV, K_A)
    adj_wts = adj_weight.reshape(SHARDS, FBLK_DEV, BLK, K_A * BLK)
    slot_ids = interp_slot.reshape(SHARDS, FBLK_DEV, K_I)
    interp_wts = interp_weight.reshape(SHARDS, FBLK_DEV, BLK, K_I * BLK)
    sources = jnp.arange(SHARDS, dtype=jnp.int32)
    global_ids = sources[:, None, None] * CBLK_DEV + coarse_send
    slot_table = jnp.transpose(global_ids, (1, 0, 2)).reshape(SHARDS, SHARDS * SLOTS)

    def interp_one(device):
        coarse_ids = slot_table[device][slot_ids[device]]
        coarse_rows = coarse_latent[coarse_ids].reshape(FBLK_DEV, K_I * BLK, LAT)
        mixed = jnp.einsum('bim,bml->bil', interp_wts[device].astype(jnp.float32), coarse_rows.astype(jnp.float32))
        return mixed.astype(jnp.bfloat16)
    interp = lax.map(interp_one, sources)
    live_all = jnp.arange(FBLK_DEV, dtype=jnp.int32)[None, :] < block_count[:, None]
    latent = fine
    for layer_step in range(STEPS):

        def update_one(device, latent=latent, layer_step=layer_step):
            dom_index = device // N_SUB
            sub_index = device % N_SUB
            peer_ids = dom_index * N_SUB + jnp.arange(N_SUB, dtype=jnp.int32)
            sub_blocks = halo_sub_send[peer_ids, sub_index]
            got_sub = latent[peer_ids[:, None], sub_blocks].reshape(N_SUB * HS, BLK, LAT)
            below_id = jnp.maximum(device - N_SUB, 0)
            above_id = jnp.minimum(device + N_SUB, SHARDS - 1)
            from_below = latent[below_id][halo_dom_send[below_id, 0]]
            from_below = jnp.where(dom_index > 0, from_below, jnp.zeros_like(from_below))
            from_above = latent[above_id][halo_dom_send[above_id, 1]]
            from_above = jnp.where(dom_index < N_DOM - 1, from_above, jnp.zeros_like(from_above))
            block_pool = jnp.concatenate([latent[device], got_sub, from_below, from_above], axis=0)
            tile_rows = block_pool[adj_ids[device]].reshape(FBLK_DEV, K_A * BLK, LAT)
            summed = jnp.einsum('bim,bml->bil', adj_wts[device].astype(jnp.float32), tile_rows.astype(jnp.float32)).astype(jnp.bfloat16)
            return node_update(latent[device], summed, interp[device], w_in[layer_step], b_in[layer_step], w_out[layer_step], ln_gain[layer_step], live_all[device])
        latent = lax.map(update_one, sources)
    return latent.reshape(SHARDS * FBLK_DEV, BLK, LAT)
```

```python
import functools
import math

import jax
import jax.numpy as jnp
from jax import lax
from jax.experimental import pallas as pl
from jax.experimental.pallas import tpu as pltpu
from jax.sharding import PartitionSpec as P

MESH = pl.DeviceIdType.MESH


def kernel(
    n_dom,
    n_sub,
    width,
    steps,
    fine_hbm,
    coarse_hbm,
    adj_index_hbm,
    adj_hbm,
    interp_slot_hbm,
    interp_hbm,
    coarse_send_hbm,
    halo_sub_hbm,
    halo_dom_hbm,
    count_hbm,
    w_in_hbm,
    b_in_hbm,
    w_out_hbm,
    ln_gain_hbm,
    out,
    *scratch,
):
    held = scratch[:steps]
    pools = scratch[steps : 2 * steps]
    sub_outs = scratch[2 * steps : 3 * steps]
    dom_outs = scratch[3 * steps : 4 * steps]
    (
        coarse,
        adj,
        iw,
        coarse_out,
        received,
        interp,
        summed,
        partial,
        w_in,
        b_in,
        w_out,
        ln_gain,
        adj_index,
        interp_slot,
        coarse_send,
        halo_sub_send,
        halo_dom_send,
        block_count,
        load_sem,
        ready,
        c_send,
        c_recv,
        s_send,
        s_recv,
        d_send,
        d_recv,
    ) = scratch[4 * steps :]

    n = n_dom * n_sub
    layers = n_dom // width
    dom, sub = lax.axis_index("dom"), lax.axis_index("sub")
    layer, column = dom // width, dom % width
    me = dom * n_sub + sub
    n_fine, rows, lat = out.shape
    slots = coarse_out.shape[1]
    hs = sub_outs[0].shape[1]
    hd = dom_outs[0].shape[1]
    k_a, k_i = adj_index.shape[0], interp_slot.shape[0]

    barrier = pltpu.get_barrier_semaphore()

    def wrapped(position, size):
        return jnp.where(position >= size, position - size, position)

    subs = [wrapped(sub + o, n_sub) for o in range(n_sub)]
    columns = [wrapped(column + o, width) for o in range(width)]

    def greet(to, other):
        pl.semaphore_signal(barrier, inc=1, device_id=(to, other), device_id_type=MESH)

    edges = [(layer < layers - 1, dom + width), (layer > 0, dom - width)]
    if width > 1:
        edges += [
            (jnp.logical_and(column == width - 1, dom < n_dom - 1), dom + 1),
            (jnp.logical_and(column == 0, dom > 0), dom - 1),
        ]

    for there, to in edges:

        @pl.when(there)
        def _(to=to):
            greet(to, sub)

    for c in range(width):
        for s in range(n_sub):
            if c or s:
                greet(layer * width + columns[c], subs[s])
    greeted = width * n_sub - 1
    for there, _ in edges:
        greeted = greeted + jnp.where(there, 1, 0)

    loads = [
        pltpu.make_async_copy(src, dst, load_sem.at[i])
        for i, (src, dst) in enumerate(
            [
                (fine_hbm, held[0]),
                (halo_dom_hbm, halo_dom_send),
                (halo_sub_hbm, halo_sub_send),
                (coarse_send_hbm, coarse_send),
                (coarse_hbm, coarse),
                (adj_index_hbm, adj_index),
                (interp_slot_hbm, interp_slot),
                (count_hbm, block_count),
                (adj_hbm, adj),
                (interp_hbm, iw),
                (w_in_hbm, w_in),
                (b_in_hbm, b_in),
                (w_out_hbm, w_out),
                (ln_gain_hbm, ln_gain),
            ]
        )
    ]
    for copy in loads[:8]:
        copy.start()

    def gather_sub(t):
        for i in range(n_sub):
            for s in range(hs):
                sub_outs[t][i, s] = held[t][halo_sub_send[0, i, s]]

    def gather_dom(t):
        for i in range(2):
            for s in range(hd):
                dom_outs[t][i, s] = held[t][halo_dom_send[0, i, s]]

    def sub_copy(t, peer, owner):
        return pltpu.make_async_remote_copy(
            src_ref=sub_outs[t].at[peer],
            dst_ref=pools[t].at[pl.ds(n_fine + owner * hs, hs)],
            send_sem=s_send.at[t],
            recv_sem=s_recv.at[t],
            device_id=(dom, peer),
            device_id_type=MESH,
        )

    def dom_copy(t, way):
        target = dom + 1 if way == 0 else dom - 1
        return pltpu.make_async_remote_copy(
            src_ref=dom_outs[t].at[way],
            dst_ref=pools[t].at[pl.ds(n_fine + n_sub * hs + way * hd, hd)],
            send_sem=d_send.at[t, way],
            recv_sem=d_recv.at[t, way],
            device_id=(target, sub),
            device_id_type=MESH,
        )

    def coarse_copy(to, other):
        return pltpu.make_async_remote_copy(
            src_ref=coarse_out.at[to * n_sub + other],
            dst_ref=received.at[pl.ds(me * slots, slots)],
            send_sem=c_send,
            recv_sem=c_recv,
            device_id=(to, other),
            device_id_type=MESH,
        )

    def all_of(ref, blocks, sem):
        part = ref.at[pl.ds(0, blocks)]
        return pltpu.make_async_copy(part, part, sem)

    def start_dom(t, way):
        @pl.when(dom < n_dom - 1 if way == 0 else dom > 0)
        def _():
            dom_copy(t, way).start()

    def start_sub(t):
        for o in range(1, n_sub):
            sub_copy(t, subs[o], sub).start()

    def local_pool(t):
        pools[t][pl.ds(n_fine + sub * hs, hs)] = sub_outs[t][sub]
        base = n_fine + n_sub * hs

        @pl.when(dom == 0)
        def _():
            pools[t][pl.ds(base, hd)] = jnp.zeros((hd, rows, lat), pools[t].dtype)

        @pl.when(dom == n_dom - 1)
        def _():
            pools[t][pl.ds(base + hd, hd)] = jnp.zeros((hd, rows, lat), pools[t].dtype)

    def wait_halo(t):
        all_of(pools[t], (n_sub - 1) * hs, s_recv.at[t]).wait()

        @pl.when(dom > 0)
        def _():
            dom_copy(t, 0).wait_recv()

        @pl.when(dom < n_dom - 1)
        def _():
            dom_copy(t, 1).wait_recv()

    def finish_halo_sends(t):
        all_of(pools[t], (n_sub - 1) * hs, s_send.at[t]).wait()

        @pl.when(dom < n_dom - 1)
        def _():
            dom_copy(t, 0).wait_send()

        @pl.when(dom > 0)
        def _():
            dom_copy(t, 1).wait_send()

    with jax.named_scope("A_load"):
        for copy in loads[:3]:
            copy.wait()
        gather_dom(0)
    with jax.named_scope("B_barrier"):
        pl.semaphore_wait(barrier, greeted)

    def tell(about):
        return lambda to: pl.semaphore_signal(
            ready.at[about], inc=1, device_id=(to, sub), device_id_type=MESH
        )

    @pl.when(layer < layers - 1)
    def _():
        tell(layer)(dom + width)

    @pl.when(layer > 0)
    def _():
        tell(layer)(dom - width)

    with jax.named_scope("C_halo"):
        start_dom(0, 0)
        start_dom(0, 1)
        gather_sub(0)
        start_sub(0)
    for copy in loads[8:]:
        copy.start()
    with jax.named_scope("D_gcoarse"):
        loads[3].wait()
        loads[4].wait()

        def gather_coarse(d, _):
            for s in range(slots):
                coarse_out[d, s] = coarse[coarse_send[0, s, d]]
            return 0

        lax.fori_loop(0, n, gather_coarse, 0, unroll=4)
        received[pl.ds(me * slots, slots)] = coarse_out[me]

    def send_layer(to_layer, skip):
        for c in range(width):
            for s in range(n_sub):
                if c or s or not skip:
                    coarse_copy(to_layer * width + columns[c], subs[s]).start()

    with jax.named_scope("E_ready"):
        for k in range(1, layers):

            @pl.when(layer >= k)
            def _():
                pl.semaphore_wait(ready.at[layer - k], 1)

                @pl.when(layer < layers - 1)
                def _():
                    tell(layer - k)(dom + width)

                send_layer(layer - k, False)

            @pl.when(layer + k < layers)
            def _():
                pl.semaphore_wait(ready.at[layer + k], 1)

                @pl.when(layer > 0)
                def _():
                    tell(layer + k)(dom - width)

                send_layer(layer + k, False)

        send_layer(layer, True)

    for copy in loads[5:8]:
        copy.wait()
    pools[0][pl.ds(0, n_fine)] = held[0][...]
    local_pool(0)

    live = block_count[0]
    chunk = math.gcd(n_fine, 16)

    def matmul(x, w):
        return jnp.dot(x, w, preferred_element_type=jnp.float32)

    def product(weights, table, index, tiles, b):
        picked = jnp.concatenate([table[index[k, b]] for k in range(tiles)], axis=0)
        return matmul(weights[b], picked).astype(jnp.bfloat16)

    def flat(ref, at):
        return ref[at].reshape(-1, lat)

    def second_layer(t):
        wide = w_out[t].astype(jnp.float32)
        wide = wide - jnp.mean(wide, axis=-1, keepdims=True)
        high = wide.astype(jnp.bfloat16)
        low = (wide - high.astype(jnp.float32)).astype(jnp.bfloat16)
        return jnp.concatenate([high, low], axis=1)

    def finish(t, h, hidden, split):
        ones = jnp.ones((lat, lat), jnp.bfloat16)
        hidden = jnp.maximum(hidden, 0.0).astype(jnp.bfloat16)
        halves = matmul(hidden, split)
        centred = halves[:, :lat] + halves[:, lat:]
        squares = (centred * centred).astype(jnp.bfloat16)
        variance = matmul(squares, ones) * (1.0 / lat)
        normed = centred * lax.rsqrt(variance + 1e-05) * ln_gain[pl.ds(t, 1)]
        return h.astype(jnp.float32) + normed

    def alive(updated, c):
        shape = (chunk, rows, lat)
        block = c * chunk + lax.broadcasted_iota(jnp.int32, shape, 0)
        updated = updated.reshape(shape)
        return jnp.where(block < live, updated, 0.0).astype(out.dtype)

    def chunks(body):
        def step(c, _):
            body(c, pl.ds(c * chunk, chunk))
            return 0

        lax.fori_loop(0, n_fine // chunk, step, 0)

    for t in range(steps):
        with jax.named_scope("F_weights"):
            if t == 0:
                for copy in loads[10:]:
                    copy.wait()
            split = second_layer(t)
            w_own = w_in[t, :lat]
            w_sum = w_in[t, lat : 2 * lat]
            w_interp = w_in[t, 2 * lat :]
            w_ends = jnp.concatenate([w_own, w_interp], axis=0)
            bias = b_in[pl.ds(t, 1)]
        if t > 0:
            with jax.named_scope("G_pre"):

                def before(c, at):
                    ends = jnp.concatenate([flat(held[t], at), flat(interp, at)], axis=1)
                    partial[at] = (matmul(ends, w_ends) + bias).reshape(chunk, rows, lat)

                chunks(before)
        with jax.named_scope("H_waithalo"):
            wait_halo(t)
            if t == 0:
                loads[8].wait()
        with jax.named_scope("I_product"):

            def gathered(c, at):
                for u in range(chunk):
                    b = c * chunk + u
                    summed[b] = product(adj, pools[t], adj_index, k_a, b)
                if t == 0:
                    ends = jnp.concatenate([flat(held[t], at), flat(summed, at)], axis=1)
                    w_first = w_in[t, : 2 * lat]
                    partial[at] = (matmul(ends, w_first) + bias).reshape(chunk, rows, lat)
                else:
                    hidden = flat(partial, at) + matmul(flat(summed, at), w_sum)
                    updated = alive(finish(t, flat(held[t], at), hidden, split), c)
                    if t == steps - 1:
                        out[at] = updated
                    else:
                        held[t + 1][at] = updated

            chunks(gathered)
        if t == 0:
            with jax.named_scope("J_waitcoarse"):
                loads[9].wait()
                all_of(received, (n - 1) * slots, c_recv).wait()
            if steps > 1:
                with jax.named_scope("K_early"):
                    for way in range(2):
                        picks = [halo_dom_send[0, way, s] for s in range(hd)]
                        mixed = jnp.concatenate(
                            [product(iw, received, interp_slot, k_i, g) for g in picks]
                        )
                        hidden = jnp.concatenate([partial[g] for g in picks])
                        own = jnp.concatenate([held[0][g] for g in picks])
                        updated = finish(0, own, hidden + matmul(mixed, w_interp), split)
                        for s, g in enumerate(picks):
                            one = updated[s * rows : (s + 1) * rows]
                            one = jnp.where(g < live, one, 0.0)
                            dom_outs[1][way, s] = one.astype(out.dtype)
                        start_dom(1, way)
            with jax.named_scope("L_update"):

                def interpolated(c, at):
                    for u in range(chunk):
                        b = c * chunk + u
                        interp[b] = product(iw, received, interp_slot, k_i, b)
                    hidden = flat(partial, at) + matmul(flat(interp, at), w_interp)
                    updated = alive(finish(t, flat(held[t], at), hidden, split), c)
                    if steps == 1:
                        out[at] = updated
                    else:
                        held[1][at] = updated

                chunks(interpolated)
        if t < steps - 1:
            with jax.named_scope("M_send"):
                if t > 0:
                    gather_dom(t + 1)
                    start_dom(t + 1, 0)
                    start_dom(t + 1, 1)
                gather_sub(t + 1)
                start_sub(t + 1)
                pools[t + 1][pl.ds(0, n_fine)] = held[t + 1][...]
                local_pool(t + 1)

    with jax.named_scope("N_finish"):
        for t in range(steps):
            finish_halo_sends(t)
        all_of(received, (n - 1) * slots, c_send).wait()


def per_device(
    n_dom,
    n_sub,
    fine_latent,
    coarse_latent,
    adj_index,
    adj_weight,
    interp_slot,
    interp_weight,
    coarse_send,
    halo_sub_send,
    halo_dom_send,
    block_count,
    w_in,
    b_in,
    w_out,
    ln_gain,
):
    n = n_dom * n_sub
    width = max(w for w in range(1, n_dom + 1) if n_dom % w == 0 and w * w <= n_dom)
    steps = w_in.shape[0]
    n_fine, rows, lat = fine_latent.shape
    slots = coarse_send.shape[2]
    hs, hd = halo_sub_send.shape[2], halo_dom_send.shape[2]
    pool = n_fine + n_sub * hs + 2 * hd
    kind = fine_latent.dtype

    def vmem(*lead):
        return pltpu.VMEM(lead + (rows, lat), kind)

    dma = pltpu.SemaphoreType.DMA
    args = (
        fine_latent,
        coarse_latent,
        adj_index.T,
        adj_weight,
        interp_slot.T,
        interp_weight,
        coarse_send.transpose(0, 2, 1),
        halo_sub_send,
        halo_dom_send,
        block_count,
        w_in,
        b_in,
        w_out,
        ln_gain,
    )
    scratch = (
        [vmem(n_fine)] * steps
        + [vmem(pool)] * steps
        + [vmem(n_sub, hs)] * steps
        + [vmem(2, hd)] * steps
        + [
            pltpu.VMEM(coarse_latent.shape, kind),
            pltpu.VMEM(adj_weight.shape, kind),
            pltpu.VMEM(interp_weight.shape, kind),
            vmem(n, slots),
            vmem(n * slots),
            vmem(n_fine),
            vmem(n_fine),
            pltpu.VMEM((n_fine, rows, lat), jnp.float32),
            pltpu.VMEM(w_in.shape, w_in.dtype),
            pltpu.VMEM(b_in.shape, b_in.dtype),
            pltpu.VMEM(w_out.shape, w_out.dtype),
            pltpu.VMEM(ln_gain.shape, ln_gain.dtype),
        ]
        + [pltpu.SMEM(args[i].shape, jnp.int32) for i in (2, 4, 6, 7, 8, 9)]
        + [
            dma((14,)),
            pltpu.SemaphoreType.REGULAR((n_dom // width,)),
            dma,
            dma,
            dma((steps,)),
            dma((steps,)),
            dma((steps, 2)),
            dma((steps, 2)),
        ]
    )
    hbm = pl.BlockSpec(memory_space=pltpu.HBM)
    return pl.pallas_call(
        functools.partial(kernel, n_dom, n_sub, width, steps),
        out_shape=pltpu.VMEM(fine_latent.shape, kind),
        in_specs=[hbm] * 14,
        scratch_shapes=scratch,
        compiler_params=pltpu.CompilerParams(
            collective_id=0, has_side_effects=True, vmem_limit_bytes=67043328 - fine_latent.size * 2
        ),
        name="graph_steps",
    )(*args)


def solution(mesh):
    placed = (
        P(("dom", "sub"), None, None),
        P(("dom", "sub"), None, None),
        P(("dom", "sub"), None),
        P(("dom", "sub"), None, None),
        P(("dom", "sub"), None),
        P(("dom", "sub"), None, None),
        P(("dom", "sub"), None, None),
        P(("dom", "sub"), None, None),
        P(("dom", "sub"), None, None),
        P(("dom", "sub")),
        P(),
        P(),
        P(),
        P(),
    )
    return jax.shard_map(
        functools.partial(per_device, mesh.shape["dom"], mesh.shape["sub"]),
        mesh=mesh,
        in_specs=placed,
        out_specs=P(("dom", "sub"), None, None),
        check_vma=False,
    )
```

```python
import functools
import math

import jax
import jax.numpy as jnp
from jax import lax
from jax.experimental import pallas as pl
from jax.experimental.pallas import tpu as pltpu
from jax.sharding import PartitionSpec as P

MESH = pl.DeviceIdType.MESH


def kernel(
    n_dom,
    n_sub,
    width,
    steps,
    fine_hbm,
    coarse_hbm,
    adj_index_hbm,
    adj_hbm,
    interp_slot_hbm,
    interp_hbm,
    coarse_send_hbm,
    halo_sub_hbm,
    halo_dom_hbm,
    count_hbm,
    w_in_hbm,
    b_in_hbm,
    w_out_hbm,
    ln_gain_hbm,
    out,
    *scratch,
):
    held = scratch[:steps]
    pools = scratch[steps : 2 * steps]
    sub_outs = scratch[2 * steps : 3 * steps]
    dom_outs = scratch[3 * steps : 4 * steps]
    (
        coarse,
        adj,
        iw,
        coarse_out,
        received,
        relay_in,
        relay_out,
        interp,
        summed,
        partial,
        w_in,
        b_in,
        w_out,
        ln_gain,
        adj_index,
        interp_slot,
        coarse_send,
        halo_sub_send,
        halo_dom_send,
        block_count,
        relay_send,
        load_sem,
        ready,
        r_send,
        r_recv,
        c_send,
        c_recv,
        s_send,
        s_recv,
        d_send,
        d_recv,
    ) = scratch[4 * steps :]

    n = n_dom * n_sub
    layers = n_dom // width
    middle = layers // 2
    dom, sub = lax.axis_index("dom"), lax.axis_index("sub")
    layer, column = dom // width, dom % width
    me = dom * n_sub + sub
    n_fine, rows, lat = out.shape
    slots = coarse_out.shape[1]
    hs = sub_outs[0].shape[1]
    hd = dom_outs[0].shape[1]
    k_a, k_i = adj_index.shape[0], interp_slot.shape[0]

    barrier = pltpu.get_barrier_semaphore()

    def wrapped(position, size):
        return jnp.where(position >= size, position - size, position)

    subs = [wrapped(sub + o, n_sub) for o in range(n_sub)]
    columns = [wrapped(column + o, width) for o in range(width)]

    def greet(to, other):
        pl.semaphore_signal(barrier, inc=1, device_id=(to, other), device_id_type=MESH)

    edges = [(layer < layers - 1, dom + width), (layer > 0, dom - width)]
    if width > 1:
        edges += [
            (jnp.logical_and(column == width - 1, dom < n_dom - 1), dom + 1),
            (jnp.logical_and(column == 0, dom > 0), dom - 1),
        ]

    for there, to in edges:

        @pl.when(there)
        def _(to=to):
            greet(to, sub)

    for c in range(width):
        for s in range(n_sub):
            if c or s:
                greet(layer * width + columns[c], subs[s])
    greeted = width * n_sub - 1
    for there, _ in edges:
        greeted = greeted + jnp.where(there, 1, 0)

    loads = [
        pltpu.make_async_copy(src, dst, load_sem.at[i])
        for i, (src, dst) in enumerate(
            [
                (fine_hbm, held[0]),
                (halo_dom_hbm, halo_dom_send),
                (halo_sub_hbm, halo_sub_send),
                (coarse_send_hbm, coarse_send),
                (coarse_hbm, coarse),
                (adj_index_hbm, adj_index),
                (interp_slot_hbm, interp_slot),
                (count_hbm, block_count),
                (adj_hbm, adj),
                (interp_hbm, iw),
                (w_in_hbm, w_in),
                (b_in_hbm, b_in),
                (w_out_hbm, w_out),
                (ln_gain_hbm, ln_gain),
            ]
        )
    ]
    for copy in loads[:8]:
        copy.start()

    def gather_sub(t):
        for i in range(n_sub):
            for s in range(hs):
                sub_outs[t][i, s] = held[t][halo_sub_send[0, i, s]]

    def gather_dom(t):
        for i in range(2):
            for s in range(hd):
                dom_outs[t][i, s] = held[t][halo_dom_send[0, i, s]]

    def sub_copy(t, peer, owner):
        return pltpu.make_async_remote_copy(
            src_ref=sub_outs[t].at[peer],
            dst_ref=pools[t].at[pl.ds(n_fine + owner * hs, hs)],
            send_sem=s_send.at[t],
            recv_sem=s_recv.at[t],
            device_id=(dom, peer),
            device_id_type=MESH,
        )

    def dom_copy(t, way):
        target = dom + 1 if way == 0 else dom - 1
        return pltpu.make_async_remote_copy(
            src_ref=dom_outs[t].at[way],
            dst_ref=pools[t].at[pl.ds(n_fine + n_sub * hs + way * hd, hd)],
            send_sem=d_send.at[t, way],
            recv_sem=d_recv.at[t, way],
            device_id=(target, sub),
            device_id_type=MESH,
        )

    def coarse_copy(to, other):
        return pltpu.make_async_remote_copy(
            src_ref=coarse_out.at[to * n_sub + other],
            dst_ref=received.at[pl.ds(me * slots, slots)],
            send_sem=c_send,
            recv_sem=c_recv,
            device_id=(to, other),
            device_id_type=MESH,
        )

    low, high = layer == middle - 1, layer == middle
    mate = jnp.where(low, dom + width, dom - width)
    mated = mate * n_sub + sub

    def relay_copies():
        pairs = [(coarse, relay_in), (coarse_send, relay_send)]
        return [
            pltpu.make_async_remote_copy(
                src_ref=src,
                dst_ref=dst,
                send_sem=r_send.at[i],
                recv_sem=r_recv.at[i],
                device_id=(mate, sub),
                device_id_type=MESH,
            )
            for i, (src, dst) in enumerate(pairs)
        ]

    def passed_on(to, other):
        peer = to * n_sub + other
        return pltpu.make_async_remote_copy(
            src_ref=relay_out.at[peer],
            dst_ref=received.at[pl.ds(mated * slots, slots)],
            send_sem=c_send,
            recv_sem=c_recv,
            device_id=(to, other),
            device_id_type=MESH,
        )

    def all_of(ref, blocks, sem):
        part = ref.at[pl.ds(0, blocks)]
        return pltpu.make_async_copy(part, part, sem)

    def coarse_wait(sem, blocks_low, blocks_high):
        cases = [(low, blocks_low), (high, blocks_high)]
        for case, blocks in cases if middle else []:

            @pl.when(case)
            def _():
                all_of(received, blocks * slots, sem).wait()

        @pl.when(jnp.logical_not(jnp.logical_or(low, high)) if middle else n > 0)
        def _():
            all_of(received, (n - 1) * slots, sem).wait()

    def start_dom(t, way):
        @pl.when(dom < n_dom - 1 if way == 0 else dom > 0)
        def _():
            dom_copy(t, way).start()

    def start_sub(t):
        for o in range(1, n_sub):
            sub_copy(t, subs[o], sub).start()

    def local_pool(t):
        pools[t][pl.ds(n_fine + sub * hs, hs)] = sub_outs[t][sub]
        base = n_fine + n_sub * hs

        @pl.when(dom == 0)
        def _():
            pools[t][pl.ds(base, hd)] = jnp.zeros((hd, rows, lat), pools[t].dtype)

        @pl.when(dom == n_dom - 1)
        def _():
            pools[t][pl.ds(base + hd, hd)] = jnp.zeros((hd, rows, lat), pools[t].dtype)

    def wait_halo(t):
        all_of(pools[t], (n_sub - 1) * hs, s_recv.at[t]).wait()

        @pl.when(dom > 0)
        def _():
            dom_copy(t, 0).wait_recv()

        @pl.when(dom < n_dom - 1)
        def _():
            dom_copy(t, 1).wait_recv()

    def finish_halo_sends(t):
        all_of(pools[t], (n_sub - 1) * hs, s_send.at[t]).wait()

        @pl.when(dom < n_dom - 1)
        def _():
            dom_copy(t, 0).wait_send()

        @pl.when(dom > 0)
        def _():
            dom_copy(t, 1).wait_send()

    with jax.named_scope("A_load"):
        for copy in loads[:3]:
            copy.wait()
        gather_dom(0)
    with jax.named_scope("B_barrier"):
        pl.semaphore_wait(barrier, greeted)

    def tell(about):
        return lambda to: pl.semaphore_signal(
            ready.at[about], inc=1, device_id=(to, sub), device_id_type=MESH
        )

    @pl.when(layer < layers - 1)
    def _():
        tell(layer)(dom + width)

    @pl.when(layer > 0)
    def _():
        tell(layer)(dom - width)

    with jax.named_scope("C_halo"):
        loads[3].wait()
        loads[4].wait()

        @pl.when(jnp.logical_or(low, high))
        def _():
            for copy in relay_copies():
                copy.start()

        start_dom(0, 0)
        start_dom(0, 1)
        gather_sub(0)
        start_sub(0)
    for copy in loads[8:]:
        copy.start()
    with jax.named_scope("D_gcoarse"):

        def gather_coarse(d, _):
            for s in range(slots):
                coarse_out[d, s] = coarse[coarse_send[0, s, d]]
            return 0

        lax.fori_loop(0, n, gather_coarse, 0, unroll=4)
        received[pl.ds(me * slots, slots)] = coarse_out[me]

    def send_layer(to_layer, skip, copy):
        for c in range(width):
            for s in range(n_sub):
                if c or s or not skip:
                    copy(to_layer * width + columns[c], subs[s]).start()

    def direct(to_layer):
        across = jnp.where(to_layer < middle, high, low)

        @pl.when(jnp.logical_not(across))
        def _():
            send_layer(to_layer, False, coarse_copy)

    with jax.named_scope("E_ready"):
        for k in range(1, layers):

            @pl.when(layer >= k)
            def _():
                pl.semaphore_wait(ready.at[layer - k], 1)

                @pl.when(layer < layers - 1)
                def _():
                    tell(layer - k)(dom + width)

                direct(layer - k)

            @pl.when(layer + k < layers)
            def _():
                pl.semaphore_wait(ready.at[layer + k], 1)

                @pl.when(layer > 0)
                def _():
                    tell(layer + k)(dom - width)

                direct(layer + k)

        send_layer(layer, True, coarse_copy)

    half = width * n_sub

    def relay(first, last):
        for copy in relay_copies():
            copy.wait_recv()

        def gather_relay(d, _):
            for s in range(slots):
                relay_out[d, s] = relay_in[relay_send[0, s, d]]
            return 0

        lax.fori_loop(first * half, last * half, gather_relay, 0, unroll=4)
        for away in range(1, last - first):
            send_layer(layer + away if first else layer - away, False, passed_on)
        send_layer(layer, True, passed_on)
        received[pl.ds(mated * slots, slots)] = relay_out[me]

    with jax.named_scope("F_relay"):
        if middle:

            @pl.when(low)
            def _():
                relay(0, middle)

            @pl.when(high)
            def _():
                relay(middle, layers)

    for copy in loads[5:8]:
        copy.wait()
    pools[0][pl.ds(0, n_fine)] = held[0][...]
    local_pool(0)

    live = block_count[0]
    chunk = math.gcd(n_fine, 16)

    def matmul(x, w):
        return jnp.dot(x, w, preferred_element_type=jnp.float32)

    def product(weights, table, index, tiles, b):
        picked = jnp.concatenate([table[index[k, b]] for k in range(tiles)], axis=0)
        return matmul(weights[b], picked).astype(jnp.bfloat16)

    def flat(ref, at):
        return ref[at].reshape(-1, lat)

    def second_layer(t):
        wide = w_out[t].astype(jnp.float32)
        wide = wide - jnp.mean(wide, axis=-1, keepdims=True)
        high = wide.astype(jnp.bfloat16)
        low = (wide - high.astype(jnp.float32)).astype(jnp.bfloat16)
        return jnp.concatenate([high, low], axis=1)

    def finish(t, h, hidden, split):
        ones = jnp.ones((lat, lat), jnp.bfloat16)
        hidden = jnp.maximum(hidden, 0.0).astype(jnp.bfloat16)
        halves = matmul(hidden, split)
        centred = halves[:, :lat] + halves[:, lat:]
        squares = (centred * centred).astype(jnp.bfloat16)
        variance = matmul(squares, ones) * (1.0 / lat)
        normed = centred * lax.rsqrt(variance + 1e-05) * ln_gain[pl.ds(t, 1)]
        return h.astype(jnp.float32) + normed

    def alive(updated, c):
        shape = (chunk, rows, lat)
        block = c * chunk + lax.broadcasted_iota(jnp.int32, shape, 0)
        updated = updated.reshape(shape)
        return jnp.where(block < live, updated, 0.0).astype(out.dtype)

    def chunks(body):
        def step(c, _):
            body(c, pl.ds(c * chunk, chunk))
            return 0

        lax.fori_loop(0, n_fine // chunk, step, 0)

    for t in range(steps):
        with jax.named_scope("F_weights"):
            if t == 0:
                for copy in loads[10:]:
                    copy.wait()
            split = second_layer(t)
            w_own = w_in[t, :lat]
            w_sum = w_in[t, lat : 2 * lat]
            w_interp = w_in[t, 2 * lat :]
            w_ends = jnp.concatenate([w_own, w_interp], axis=0)
            bias = b_in[pl.ds(t, 1)]
        if t > 0:
            with jax.named_scope("G_pre"):

                def before(c, at):
                    ends = jnp.concatenate([flat(held[t], at), flat(interp, at)], axis=1)
                    partial[at] = (matmul(ends, w_ends) + bias).reshape(chunk, rows, lat)

                chunks(before)
        with jax.named_scope("H_waithalo"):
            wait_halo(t)
            if t == 0:
                loads[8].wait()
        with jax.named_scope("I_product"):

            def gathered(c, at):
                for u in range(chunk):
                    b = c * chunk + u
                    summed[b] = product(adj, pools[t], adj_index, k_a, b)
                if t == 0:
                    ends = jnp.concatenate([flat(held[t], at), flat(summed, at)], axis=1)
                    w_first = w_in[t, : 2 * lat]
                    partial[at] = (matmul(ends, w_first) + bias).reshape(chunk, rows, lat)
                else:
                    hidden = flat(partial, at) + matmul(flat(summed, at), w_sum)
                    updated = alive(finish(t, flat(held[t], at), hidden, split), c)
                    if t == steps - 1:
                        out[at] = updated
                    else:
                        held[t + 1][at] = updated

            chunks(gathered)
        if t == 0:
            with jax.named_scope("J_waitcoarse"):
                loads[9].wait()
                coarse_wait(c_recv, n - 2, n - 2)
            if steps > 1:
                with jax.named_scope("K_early"):
                    def early(picks):
                        mixed = jnp.concatenate(
                            [product(iw, received, interp_slot, k_i, g) for g in picks]
                        )
                        hidden = jnp.concatenate([partial[g] for g in picks])
                        own = jnp.concatenate([held[0][g] for g in picks])
                        updated = finish(0, own, hidden + matmul(mixed, w_interp), split)
                        for i, g in enumerate(picks):
                            one = updated[i * rows : (i + 1) * rows]
                            yield jnp.where(g < live, one, 0.0).astype(out.dtype)

                    for way in range(2):
                        picks = [halo_dom_send[0, way, s] for s in range(hd)]
                        for s, one in enumerate(early(picks)):
                            dom_outs[1][way, s] = one
                        start_dom(1, way)
                    places = [(subs[o], s) for o in range(1, n_sub) for s in range(hs)]
                    picks = [halo_sub_send[0, peer, s] for peer, s in places]
                    for (peer, s), one in zip(places, early(picks)):
                        sub_outs[1][peer, s] = one
                    start_sub(1)
            with jax.named_scope("L_update"):

                def interpolated(c, at):
                    for u in range(chunk):
                        b = c * chunk + u
                        interp[b] = product(iw, received, interp_slot, k_i, b)
                    hidden = flat(partial, at) + matmul(flat(interp, at), w_interp)
                    updated = alive(finish(t, flat(held[t], at), hidden, split), c)
                    if steps == 1:
                        out[at] = updated
                    else:
                        held[1][at] = updated

                chunks(interpolated)
        if t < steps - 1:
            with jax.named_scope("M_send"):
                if t > 0:
                    gather_dom(t + 1)
                    start_dom(t + 1, 0)
                    start_dom(t + 1, 1)
                if t > 0:
                    gather_sub(t + 1)
                    start_sub(t + 1)
                else:
                    for s in range(hs):
                        sub_outs[1][sub, s] = held[1][halo_sub_send[0, sub, s]]
                pools[t + 1][pl.ds(0, n_fine)] = held[t + 1][...]
                local_pool(t + 1)

    with jax.named_scope("N_finish"):
        for t in range(steps):
            finish_halo_sends(t)
        coarse_wait(c_send, 2 * middle * half - 2, 2 * (layers - middle) * half - 2)

        @pl.when(jnp.logical_or(low, high))
        def _():
            for copy in relay_copies():
                copy.wait_send()


def per_device(
    n_dom,
    n_sub,
    fine_latent,
    coarse_latent,
    adj_index,
    adj_weight,
    interp_slot,
    interp_weight,
    coarse_send,
    halo_sub_send,
    halo_dom_send,
    block_count,
    w_in,
    b_in,
    w_out,
    ln_gain,
):
    n = n_dom * n_sub
    width = max(w for w in range(1, n_dom + 1) if n_dom % w == 0 and w * w <= n_dom)
    steps = w_in.shape[0]
    n_fine, rows, lat = fine_latent.shape
    slots = coarse_send.shape[2]
    hs, hd = halo_sub_send.shape[2], halo_dom_send.shape[2]
    pool = n_fine + n_sub * hs + 2 * hd
    kind = fine_latent.dtype

    def vmem(*lead):
        return pltpu.VMEM(lead + (rows, lat), kind)

    dma = pltpu.SemaphoreType.DMA
    args = (
        fine_latent,
        coarse_latent,
        adj_index.T,
        adj_weight,
        interp_slot.T,
        interp_weight,
        coarse_send.transpose(0, 2, 1),
        halo_sub_send,
        halo_dom_send,
        block_count,
        w_in,
        b_in,
        w_out,
        ln_gain,
    )
    scratch = (
        [vmem(n_fine)] * steps
        + [vmem(pool)] * steps
        + [vmem(n_sub, hs)] * steps
        + [vmem(2, hd)] * steps
        + [
            pltpu.VMEM(coarse_latent.shape, kind),
            pltpu.VMEM(adj_weight.shape, kind),
            pltpu.VMEM(interp_weight.shape, kind),
            vmem(n, slots),
            vmem(n * slots),
            pltpu.VMEM(coarse_latent.shape, kind),
            vmem(n, slots),
            vmem(n_fine),
            vmem(n_fine),
            pltpu.VMEM((n_fine, rows, lat), jnp.float32),
            pltpu.VMEM(w_in.shape, w_in.dtype),
            pltpu.VMEM(b_in.shape, b_in.dtype),
            pltpu.VMEM(w_out.shape, w_out.dtype),
            pltpu.VMEM(ln_gain.shape, ln_gain.dtype),
        ]
        + [pltpu.SMEM(args[i].shape, jnp.int32) for i in (2, 4, 6, 7, 8, 9, 6)]
        + [
            dma((14,)),
            pltpu.SemaphoreType.REGULAR((n_dom // width,)),
            dma((2,)),
            dma((2,)),
            dma,
            dma,
            dma((steps,)),
            dma((steps,)),
            dma((steps, 2)),
            dma((steps, 2)),
        ]
    )
    hbm = pl.BlockSpec(memory_space=pltpu.HBM)
    return pl.pallas_call(
        functools.partial(kernel, n_dom, n_sub, width, steps),
        out_shape=pltpu.VMEM(fine_latent.shape, kind),
        in_specs=[hbm] * 14,
        scratch_shapes=scratch,
        compiler_params=pltpu.CompilerParams(
            collective_id=0, has_side_effects=True, vmem_limit_bytes=67043328 - fine_latent.size * 2
        ),
        name="graph_steps",
    )(*args)


def solution(mesh):
    placed = (
        P(("dom", "sub"), None, None),
        P(("dom", "sub"), None, None),
        P(("dom", "sub"), None),
        P(("dom", "sub"), None, None),
        P(("dom", "sub"), None),
        P(("dom", "sub"), None, None),
        P(("dom", "sub"), None, None),
        P(("dom", "sub"), None, None),
        P(("dom", "sub"), None, None),
        P(("dom", "sub")),
        P(),
        P(),
        P(),
        P(),
    )
    return jax.shard_map(
        functools.partial(per_device, mesh.shape["dom"], mesh.shape["sub"]),
        mesh=mesh,
        in_specs=placed,
        out_specs=P(("dom", "sub"), None, None),
        check_vma=False,
    )
```

```python
import functools
import math

import jax
import jax.numpy as jnp
from jax import lax
from jax.experimental import pallas as pl
from jax.experimental.pallas import tpu as pltpu
from jax.sharding import PartitionSpec as P

MESH = pl.DeviceIdType.MESH


def kernel(
    n_dom,
    n_sub,
    width,
    steps,
    fine_hbm,
    coarse_hbm,
    adj_index_hbm,
    adj_hbm,
    interp_slot_hbm,
    interp_hbm,
    coarse_send_hbm,
    halo_sub_hbm,
    halo_dom_hbm,
    count_hbm,
    w_in_hbm,
    b_in_hbm,
    w_out_hbm,
    ln_gain_hbm,
    out,
    *scratch,
):
    held = scratch[:steps]
    pools = scratch[steps : 2 * steps]
    sub_outs = scratch[2 * steps : 3 * steps]
    dom_outs = scratch[3 * steps : 4 * steps]
    (
        coarse,
        adj,
        iw,
        coarse_out,
        received,
        relay_in,
        relay_out,
        interp,
        partial,
        w_in,
        b_in,
        w_out,
        ln_gain,
        adj_index,
        interp_slot,
        coarse_send,
        halo_sub_send,
        halo_dom_send,
        block_count,
        relay_send,
        load_sem,
        ready,
        r_send,
        r_recv,
        c_send,
        c_recv,
        s_send,
        s_recv,
        d_send,
        d_recv,
    ) = scratch[4 * steps :]

    n = n_dom * n_sub
    layers = n_dom // width
    middle = layers // 2
    dom, sub = lax.axis_index("dom"), lax.axis_index("sub")
    layer, column = dom // width, dom % width
    me = dom * n_sub + sub
    n_fine, rows, lat = out.shape
    slots = coarse_out.shape[1]
    hs = sub_outs[0].shape[1]
    hd = dom_outs[0].shape[1]
    k_a, k_i = adj_index.shape[0], interp_slot.shape[0]

    barrier = pltpu.get_barrier_semaphore()

    def wrapped(position, size):
        return jnp.where(position >= size, position - size, position)

    subs = [wrapped(sub + o, n_sub) for o in range(n_sub)]
    columns = [wrapped(column + o, width) for o in range(width)]

    def greet(to, other):
        pl.semaphore_signal(barrier, inc=1, device_id=(to, other), device_id_type=MESH)

    edges = [(layer < layers - 1, dom + width), (layer > 0, dom - width)]
    if width > 1:
        edges += [
            (jnp.logical_and(column == width - 1, dom < n_dom - 1), dom + 1),
            (jnp.logical_and(column == 0, dom > 0), dom - 1),
        ]

    for there, to in edges:

        @pl.when(there)
        def _(to=to):
            greet(to, sub)

    for c in range(width):
        for s in range(n_sub):
            if c or s:
                greet(layer * width + columns[c], subs[s])
    greeted = width * n_sub - 1
    for there, _ in edges:
        greeted = greeted + jnp.where(there, 1, 0)

    loads = [
        pltpu.make_async_copy(src, dst, load_sem.at[i])
        for i, (src, dst) in enumerate(
            [
                (fine_hbm, held[0]),
                (halo_dom_hbm, halo_dom_send),
                (halo_sub_hbm, halo_sub_send),
                (coarse_send_hbm, coarse_send),
                (coarse_hbm, coarse),
                (adj_index_hbm, adj_index),
                (interp_slot_hbm, interp_slot),
                (count_hbm, block_count),
                (adj_hbm, adj),
                (interp_hbm, iw),
                (w_in_hbm, w_in),
                (b_in_hbm, b_in),
                (w_out_hbm, w_out),
                (ln_gain_hbm, ln_gain),
            ]
        )
    ]
    for copy in loads[:8]:
        copy.start()

    def gather_sub(t):
        for i in range(n_sub):
            for s in range(hs):
                sub_outs[t][i, s] = held[t][halo_sub_send[0, i, s]]

    def gather_dom(t):
        for i in range(2):
            for s in range(hd):
                dom_outs[t][i, s] = held[t][halo_dom_send[0, i, s]]

    def sub_copy(t, peer, owner):
        return pltpu.make_async_remote_copy(
            src_ref=sub_outs[t].at[peer],
            dst_ref=pools[t].at[pl.ds(n_fine + owner * hs, hs)],
            send_sem=s_send.at[t],
            recv_sem=s_recv.at[t],
            device_id=(dom, peer),
            device_id_type=MESH,
        )

    def dom_copy(t, way):
        target = dom + 1 - 2 * way
        return pltpu.make_async_remote_copy(
            src_ref=dom_outs[t].at[way],
            dst_ref=pools[t].at[pl.ds(n_fine + n_sub * hs + way * hd, hd)],
            send_sem=d_send.at[t, way],
            recv_sem=d_recv.at[t, way],
            device_id=(target, sub),
            device_id_type=MESH,
        )

    def coarse_copy(to, other):
        return pltpu.make_async_remote_copy(
            src_ref=coarse_out.at[to * n_sub + other],
            dst_ref=received.at[pl.ds(me * slots, slots)],
            send_sem=c_send,
            recv_sem=c_recv,
            device_id=(to, other),
            device_id_type=MESH,
        )

    low, high = layer == middle - 1, layer == middle
    mate = jnp.where(low, dom + width, dom - width)
    mated = mate * n_sub + sub

    def relay_copies():
        pairs = [(coarse, relay_in), (coarse_send, relay_send)]
        return [
            pltpu.make_async_remote_copy(
                src_ref=src,
                dst_ref=dst,
                send_sem=r_send.at[i],
                recv_sem=r_recv.at[i],
                device_id=(mate, sub),
                device_id_type=MESH,
            )
            for i, (src, dst) in enumerate(pairs)
        ]

    def passed_on(to, other):
        peer = to * n_sub + other
        return pltpu.make_async_remote_copy(
            src_ref=relay_out.at[peer],
            dst_ref=received.at[pl.ds(mated * slots, slots)],
            send_sem=c_send,
            recv_sem=c_recv,
            device_id=(to, other),
            device_id_type=MESH,
        )

    def all_of(ref, blocks, sem):
        part = ref.at[pl.ds(0, blocks)]
        return pltpu.make_async_copy(part, part, sem)

    def coarse_wait(sem, blocks_low, blocks_high):
        cases = [(low, blocks_low), (high, blocks_high)]
        for case, blocks in cases if middle else []:

            @pl.when(case)
            def _():
                all_of(received, blocks * slots, sem).wait()

        @pl.when(jnp.logical_not(jnp.logical_or(low, high)) if middle else n > 0)
        def _():
            all_of(received, (n - 1) * slots, sem).wait()

    def start_dom(t, way):
        @pl.when(jnp.where(way == 0, dom < n_dom - 1, dom > 0))
        def _():
            dom_copy(t, way).start()

    def start_sub(t):
        for o in range(1, n_sub):
            sub_copy(t, subs[o], sub).start()

    def local_pool(t):
        pools[t][pl.ds(n_fine + sub * hs, hs)] = sub_outs[t][sub]
        base = n_fine + n_sub * hs

        @pl.when(dom == 0)
        def _():
            pools[t][pl.ds(base, hd)] = jnp.zeros((hd, rows, lat), pools[t].dtype)

        @pl.when(dom == n_dom - 1)
        def _():
            pools[t][pl.ds(base + hd, hd)] = jnp.zeros((hd, rows, lat), pools[t].dtype)

    def wait_halo(t):
        all_of(pools[t], (n_sub - 1) * hs, s_recv.at[t]).wait()

        @pl.when(dom > 0)
        def _():
            dom_copy(t, 0).wait_recv()

        @pl.when(dom < n_dom - 1)
        def _():
            dom_copy(t, 1).wait_recv()

    def finish_halo_sends(t):
        all_of(pools[t], (n_sub - 1) * hs, s_send.at[t]).wait()

        @pl.when(dom < n_dom - 1)
        def _():
            dom_copy(t, 0).wait_send()

        @pl.when(dom > 0)
        def _():
            dom_copy(t, 1).wait_send()

    first_way = jnp.where(column == 0, 1, 0)
    ways = [first_way, 1 - first_way]

    with jax.named_scope("A_load"):
        for copy in loads[:3]:
            copy.wait()
        gather_dom(0)
    with jax.named_scope("B_barrier"):
        pl.semaphore_wait(barrier, greeted)

    def tell(about):
        return lambda to: pl.semaphore_signal(
            ready.at[about], inc=1, device_id=(to, sub), device_id_type=MESH
        )

    @pl.when(layer < layers - 1)
    def _():
        tell(layer)(dom + width)

    @pl.when(layer > 0)
    def _():
        tell(layer)(dom - width)

    with jax.named_scope("C_halo"):
        loads[3].wait()
        loads[4].wait()

        @pl.when(jnp.logical_or(low, high))
        def _():
            for copy in relay_copies():
                copy.start()

        for way in ways:
            start_dom(0, way)
        gather_sub(0)
        start_sub(0)
    for copy in loads[8:]:
        copy.start()
    with jax.named_scope("D_gcoarse"):

        def gather_coarse(d, _):
            for s in range(slots):
                coarse_out[d, s] = coarse[coarse_send[0, s, d]]
            return 0

        lax.fori_loop(0, n, gather_coarse, 0, unroll=4)
        received[pl.ds(me * slots, slots)] = coarse_out[me]

    def send(to_layer, which, copy, skip=False):
        for c in which:
            for s in range(n_sub):
                if c or s or not skip:
                    copy(to_layer * width + columns[c], subs[s]).start()

    def direct(to_layer, which):
        across = jnp.where(to_layer < middle, high, low)

        @pl.when(jnp.logical_not(across))
        def _():
            send(to_layer, which, coarse_copy)

    here, aside = range(1), range(1, width)

    with jax.named_scope("E_ready"):
        for k in range(1, layers):

            @pl.when(layer >= k)
            def _():
                pl.semaphore_wait(ready.at[layer - k], 1)

                @pl.when(layer < layers - 1)
                def _():
                    tell(layer - k)(dom + width)

                direct(layer - k, here)

            @pl.when(layer + k < layers)
            def _():
                pl.semaphore_wait(ready.at[layer + k], 1)

                @pl.when(layer > 0)
                def _():
                    tell(layer + k)(dom - width)

                direct(layer + k, here)

        for k in reversed(range(1, layers)):

            @pl.when(layer >= k)
            def _():
                direct(layer - k, aside)

            @pl.when(layer + k < layers)
            def _():
                direct(layer + k, aside)

        send(layer, here, coarse_copy, True)
        send(layer, aside, coarse_copy)

    half = width * n_sub

    def relay(first, last):
        for copy in relay_copies():
            copy.wait_recv()

        def gather_relay(d, _):
            for s in range(slots):
                relay_out[d, s] = relay_in[relay_send[0, s, d]]
            return 0

        lax.fori_loop(first * half, last * half, gather_relay, 0, unroll=4)
        for which in (here, aside):
            for away in range(1, last - first):
                send(layer + away if first else layer - away, which, passed_on)
            send(layer, which, passed_on, which is here)
        received[pl.ds(mated * slots, slots)] = relay_out[me]

    with jax.named_scope("F_relay"):
        if middle:

            @pl.when(low)
            def _():
                relay(0, middle)

            @pl.when(high)
            def _():
                relay(middle, layers)

    for copy in loads[5:8]:
        copy.wait()
    pools[0][pl.ds(0, n_fine)] = held[0][...]
    local_pool(0)

    live = block_count[0]
    chunk = math.gcd(n_fine, 16)

    def matmul(x, w):
        return jnp.dot(x, w, preferred_element_type=jnp.float32)

    def product(weights, table, index, tiles, b):
        picked = jnp.concatenate([table[index[k, b]] for k in range(tiles)], axis=0)
        return matmul(weights[b], picked).astype(jnp.bfloat16)

    def flat(ref, at):
        return ref[at].reshape(-1, lat)

    def second_layer(t):
        wide = w_out[t].astype(jnp.float32)
        wide = wide - jnp.mean(wide, axis=-1, keepdims=True)
        high = wide.astype(jnp.bfloat16)
        low = (wide - high.astype(jnp.float32)).astype(jnp.bfloat16)
        return jnp.concatenate([high, low], axis=1)

    def activate(hidden):
        return jnp.maximum(hidden, 0.0).astype(jnp.bfloat16)

    def centre(hidden, split):
        halves = matmul(hidden, split)
        return halves[:, :lat] + halves[:, lat:]

    def normalize(t, h, centred):
        ones = jnp.ones((lat, lat), jnp.bfloat16)
        squares = (centred * centred).astype(jnp.bfloat16)
        variance = matmul(squares, ones) * (1.0 / lat)
        normed = centred * lax.rsqrt(variance + 1e-05) * ln_gain[pl.ds(t, 1)]
        return h.astype(jnp.float32) + normed

    def finish(t, h, hidden, split):
        return normalize(t, h, centre(activate(hidden), split))

    def staggered(pieces, stages):
        held_back = {}
        for i in range(len(pieces) + len(stages) - 1):
            for s, stage in enumerate(stages):
                if 0 <= i - s < len(pieces):
                    held_back[i - s] = stage(pieces[i - s], held_back.get(i - s))

    def alive(updated, first):
        shape = (updated.shape[0] // rows, rows, lat)
        block = first + lax.broadcasted_iota(jnp.int32, shape, 0)
        updated = updated.reshape(shape)
        return jnp.where(block < live, updated, 0.0).astype(out.dtype)

    def chunks(body):
        def step(c, _):
            body(c, pl.ds(c * chunk, chunk))
            return 0

        lax.fori_loop(0, n_fine // chunk, step, 0)

    for t in range(steps):
        with jax.named_scope("F_weights"):
            if t == 0:
                for copy in loads[10:]:
                    copy.wait()
            split = second_layer(t)
            w_own = w_in[t, :lat]
            w_sum = w_in[t, lat : 2 * lat]
            w_interp = w_in[t, 2 * lat :]
            w_ends = jnp.concatenate([w_own, w_interp], axis=0)
            bias = b_in[pl.ds(t, 1)]
        if t > 0:
            with jax.named_scope("G_pre"):

                def before(c, at):
                    ends = jnp.concatenate([flat(held[t], at), flat(interp, at)], axis=1)
                    partial[at] = (matmul(ends, w_ends) + bias).reshape(chunk, rows, lat)

                chunks(before)
        with jax.named_scope("H_waithalo"):
            wait_halo(t)
            if t == 0:
                loads[8].wait()
        with jax.named_scope("I_product"):

            size = math.gcd(n_fine, 4 if t == 0 else 4)
            pieces = range(0, n_fine, size)

            def gathered(first, _):
                blocks = range(first, first + size)
                total = [product(adj, pools[t], adj_index, k_a, b) for b in blocks]
                return jnp.concatenate(total, axis=0)

            def started(first, total):
                at = pl.ds(first, size)
                ends = jnp.concatenate([flat(held[t], at), total], axis=1)
                hidden = matmul(ends, w_in[t, : 2 * lat]) + bias
                partial[at] = hidden.reshape(size, rows, lat)

            def activated(first, total):
                at = pl.ds(first, size)
                return activate(flat(partial, at) + matmul(total, w_sum))

            def centred(first, hidden):
                return centre(hidden, split)

            def updated(first, values):
                at = pl.ds(first, size)
                values = alive(normalize(t, flat(held[t], at), values), first)
                if t == steps - 1:
                    out[at] = values
                else:
                    held[t + 1][at] = values

            if t == 0:
                staggered(pieces, [gathered, started])
            else:
                staggered(pieces, [gathered, activated, centred, updated])
        if t == 0:
            with jax.named_scope("J_waitcoarse"):
                loads[9].wait()
                coarse_wait(c_recv, n - 2, n - 2)
            if steps > 1:
                with jax.named_scope("K_early"):
                    def early(picks):
                        mixed = jnp.concatenate(
                            [product(iw, received, interp_slot, k_i, g) for g in picks]
                        )
                        hidden = jnp.concatenate([partial[g] for g in picks])
                        own = jnp.concatenate([held[0][g] for g in picks])
                        updated = finish(0, own, hidden + matmul(mixed, w_interp), split)
                        for i, g in enumerate(picks):
                            one = updated[i * rows : (i + 1) * rows]
                            yield jnp.where(g < live, one, 0.0).astype(out.dtype)

                    for way in ways:
                        picks = [halo_dom_send[0, way, s] for s in range(hd)]
                        for s, one in enumerate(early(picks)):
                            dom_outs[1][way, s] = one
                        start_dom(1, way)
                    places = [(subs[o], s) for o in range(1, n_sub) for s in range(hs)]
                    picks = [halo_sub_send[0, peer, s] for peer, s in places]
                    for (peer, s), one in zip(places, early(picks)):
                        sub_outs[1][peer, s] = one
                    start_sub(1)
            with jax.named_scope("L_update"):

                def interpolated(c, at):
                    for u in range(chunk):
                        b = c * chunk + u
                        interp[b] = product(iw, received, interp_slot, k_i, b)
                    hidden = flat(partial, at) + matmul(flat(interp, at), w_interp)
                    updated = finish(t, flat(held[t], at), hidden, split)
                    updated = alive(updated, c * chunk)
                    if steps == 1:
                        out[at] = updated
                    else:
                        held[1][at] = updated

                chunks(interpolated)
        if t < steps - 1:
            with jax.named_scope("M_send"):
                if t > 0:
                    gather_dom(t + 1)
                    for way in ways:
                        start_dom(t + 1, way)
                if t > 0:
                    gather_sub(t + 1)
                    start_sub(t + 1)
                else:
                    for s in range(hs):
                        sub_outs[1][sub, s] = held[1][halo_sub_send[0, sub, s]]
                pools[t + 1][pl.ds(0, n_fine)] = held[t + 1][...]
                local_pool(t + 1)

    with jax.named_scope("N_finish"):
        for t in range(steps):
            finish_halo_sends(t)
        coarse_wait(c_send, 2 * middle * half - 2, 2 * (layers - middle) * half - 2)

        @pl.when(jnp.logical_or(low, high))
        def _():
            for copy in relay_copies():
                copy.wait_send()


def per_device(
    n_dom,
    n_sub,
    fine_latent,
    coarse_latent,
    adj_index,
    adj_weight,
    interp_slot,
    interp_weight,
    coarse_send,
    halo_sub_send,
    halo_dom_send,
    block_count,
    w_in,
    b_in,
    w_out,
    ln_gain,
):
    n = n_dom * n_sub
    width = max(w for w in range(1, n_dom + 1) if n_dom % w == 0 and w * w <= n_dom)
    steps = w_in.shape[0]
    n_fine, rows, lat = fine_latent.shape
    slots = coarse_send.shape[2]
    hs, hd = halo_sub_send.shape[2], halo_dom_send.shape[2]
    pool = n_fine + n_sub * hs + 2 * hd
    kind = fine_latent.dtype

    def vmem(*lead):
        return pltpu.VMEM(lead + (rows, lat), kind)

    dma = pltpu.SemaphoreType.DMA
    args = (
        fine_latent,
        coarse_latent,
        adj_index.T,
        adj_weight,
        interp_slot.T,
        interp_weight,
        coarse_send.transpose(0, 2, 1),
        halo_sub_send,
        halo_dom_send,
        block_count,
        w_in,
        b_in,
        w_out,
        ln_gain,
    )
    scratch = (
        [vmem(n_fine)] * steps
        + [vmem(pool)] * steps
        + [vmem(n_sub, hs)] * steps
        + [vmem(2, hd)] * steps
        + [
            pltpu.VMEM(coarse_latent.shape, kind),
            pltpu.VMEM(adj_weight.shape, kind),
            pltpu.VMEM(interp_weight.shape, kind),
            vmem(n, slots),
            vmem(n * slots),
            pltpu.VMEM(coarse_latent.shape, kind),
            vmem(n, slots),
            vmem(n_fine),
            pltpu.VMEM((n_fine, rows, lat), jnp.float32),
            pltpu.VMEM(w_in.shape, w_in.dtype),
            pltpu.VMEM(b_in.shape, b_in.dtype),
            pltpu.VMEM(w_out.shape, w_out.dtype),
            pltpu.VMEM(ln_gain.shape, ln_gain.dtype),
        ]
        + [pltpu.SMEM(args[i].shape, jnp.int32) for i in (2, 4, 6, 7, 8, 9, 6)]
        + [
            dma((14,)),
            pltpu.SemaphoreType.REGULAR((n_dom // width,)),
            dma((2,)),
            dma((2,)),
            dma,
            dma,
            dma((steps,)),
            dma((steps,)),
            dma((steps, 2)),
            dma((steps, 2)),
        ]
    )
    hbm = pl.BlockSpec(memory_space=pltpu.HBM)
    return pl.pallas_call(
        functools.partial(kernel, n_dom, n_sub, width, steps),
        out_shape=pltpu.VMEM(fine_latent.shape, kind),
        in_specs=[hbm] * 14,
        scratch_shapes=scratch,
        compiler_params=pltpu.CompilerParams(
            collective_id=0, has_side_effects=True, vmem_limit_bytes=67043328 - fine_latent.size * 2
        ),
        name="graph_steps",
    )(*args)


def solution(mesh):
    placed = (
        P(("dom", "sub"), None, None),
        P(("dom", "sub"), None, None),
        P(("dom", "sub"), None),
        P(("dom", "sub"), None, None),
        P(("dom", "sub"), None),
        P(("dom", "sub"), None, None),
        P(("dom", "sub"), None, None),
        P(("dom", "sub"), None, None),
        P(("dom", "sub"), None, None),
        P(("dom", "sub")),
        P(),
        P(),
        P(),
        P(),
    )
    return jax.shard_map(
        functools.partial(per_device, mesh.shape["dom"], mesh.shape["sub"]),
        mesh=mesh,
        in_specs=placed,
        out_specs=P(("dom", "sub"), None, None),
        check_vma=False,
    )
```

```python
import functools
import math

import jax
import jax.numpy as jnp
from jax import lax
from jax.experimental import pallas as pl
from jax.experimental.pallas import tpu as pltpu
from jax.sharding import PartitionSpec as P

MESH = pl.DeviceIdType.MESH


def kernel(
    n_dom,
    n_sub,
    width,
    steps,
    fine_hbm,
    coarse_hbm,
    adj_index_hbm,
    adj_hbm,
    interp_slot_hbm,
    interp_hbm,
    coarse_send_hbm,
    halo_sub_hbm,
    halo_dom_hbm,
    count_hbm,
    w_in_hbm,
    b_in_hbm,
    w_out_hbm,
    ln_gain_hbm,
    out,
    *scratch,
):
    held = scratch[:steps]
    pools = scratch[steps : 2 * steps]
    sub_outs = scratch[2 * steps : 3 * steps]
    dom_outs = scratch[3 * steps : 4 * steps]
    (
        coarse,
        adj,
        iw,
        coarse_out,
        received,
        relay_in,
        relay_out,
        interp,
        partial,
        w_in,
        b_in,
        w_out,
        ln_gain,
        adj_index,
        interp_slot,
        coarse_send,
        halo_sub_send,
        halo_dom_send,
        block_count,
        relay_send,
        load_sem,
        ready,
        r_send,
        r_recv,
        c_send,
        c_recv,
        s_send,
        s_recv,
        d_send,
        d_recv,
    ) = scratch[4 * steps :]

    n = n_dom * n_sub
    layers = n_dom // width
    middle = layers // 2
    dom, sub = lax.axis_index("dom"), lax.axis_index("sub")
    layer, column = dom // width, dom % width
    me = dom * n_sub + sub
    n_fine, rows, lat = out.shape
    slots = coarse_out.shape[1]
    hs = sub_outs[0].shape[1]
    hd = dom_outs[0].shape[1]
    k_a, k_i = adj_index.shape[0], interp_slot.shape[0]

    barrier = pltpu.get_barrier_semaphore()

    def wrapped(position, size):
        return jnp.where(position >= size, position - size, position)

    subs = [wrapped(sub + o, n_sub) for o in range(n_sub)]
    columns = [wrapped(column + o, width) for o in range(width)]

    def greet(to, other):
        pl.semaphore_signal(barrier, inc=1, device_id=(to, other), device_id_type=MESH)

    edges = [(layer < layers - 1, dom + width), (layer > 0, dom - width)]
    if width > 1:
        edges += [
            (jnp.logical_and(column == width - 1, dom < n_dom - 1), dom + 1),
            (jnp.logical_and(column == 0, dom > 0), dom - 1),
        ]

    for there, to in edges:

        @pl.when(there)
        def _(to=to):
            greet(to, sub)

    for c in range(width):
        for s in range(n_sub):
            if c or s:
                greet(layer * width + columns[c], subs[s])
    greeted = width * n_sub - 1
    for there, _ in edges:
        greeted = greeted + jnp.where(there, 1, 0)

    loads = [
        pltpu.make_async_copy(src, dst, load_sem.at[i % 8])
        for i, (src, dst) in enumerate(
            [
                (fine_hbm, held[0]),
                (halo_dom_hbm, halo_dom_send),
                (halo_sub_hbm, halo_sub_send),
                (coarse_send_hbm, coarse_send),
                (coarse_hbm, coarse),
                (adj_index_hbm, adj_index),
                (interp_slot_hbm, interp_slot),
                (count_hbm, block_count),
                (adj_hbm, adj),
                (interp_hbm, iw),
                (w_in_hbm, w_in),
                (b_in_hbm, b_in),
                (w_out_hbm, w_out),
                (ln_gain_hbm, ln_gain),
            ]
        )
    ]
    for copy in loads[:8]:
        copy.start()

    def gather_sub(t):
        for i in range(n_sub):
            for s in range(hs):
                sub_outs[t][i, s] = held[t][halo_sub_send[0, i, s]]

    def gather_dom(t):
        for i in range(2):
            for s in range(hd):
                dom_outs[t][i, s] = held[t][halo_dom_send[0, i, s]]

    def sub_copy(t, peer, owner):
        return pltpu.make_async_remote_copy(
            src_ref=sub_outs[t].at[peer],
            dst_ref=pools[t].at[pl.ds(n_fine + owner * hs, hs)],
            send_sem=s_send.at[t],
            recv_sem=s_recv.at[t],
            device_id=(dom, peer),
            device_id_type=MESH,
        )

    def dom_copy(t, way):
        target = dom + 1 - 2 * way
        return pltpu.make_async_remote_copy(
            src_ref=dom_outs[t].at[way],
            dst_ref=pools[t].at[pl.ds(n_fine + n_sub * hs + way * hd, hd)],
            send_sem=d_send.at[t, way],
            recv_sem=d_recv.at[t, way],
            device_id=(target, sub),
            device_id_type=MESH,
        )

    def coarse_copy(to, other):
        return pltpu.make_async_remote_copy(
            src_ref=coarse_out.at[to * n_sub + other],
            dst_ref=received.at[pl.ds(me * slots, slots)],
            send_sem=c_send,
            recv_sem=c_recv,
            device_id=(to, other),
            device_id_type=MESH,
        )

    low, high = layer == middle - 1, layer == middle
    mate = jnp.where(low, dom + width, dom - width)
    mated = mate * n_sub + sub

    def relay_copies():
        pairs = [(coarse, relay_in), (coarse_send, relay_send)]
        return [
            pltpu.make_async_remote_copy(
                src_ref=src,
                dst_ref=dst,
                send_sem=r_send.at[i],
                recv_sem=r_recv.at[i],
                device_id=(mate, sub),
                device_id_type=MESH,
            )
            for i, (src, dst) in enumerate(pairs)
        ]

    def passed_on(to, other):
        peer = to * n_sub + other
        return pltpu.make_async_remote_copy(
            src_ref=relay_out.at[peer],
            dst_ref=received.at[pl.ds(mated * slots, slots)],
            send_sem=c_send,
            recv_sem=c_recv,
            device_id=(to, other),
            device_id_type=MESH,
        )

    def all_of(ref, blocks, sem):
        part = ref.at[pl.ds(0, blocks)]
        return pltpu.make_async_copy(part, part, sem)

    def coarse_wait(sem, blocks_low, blocks_high):
        cases = [(low, blocks_low), (high, blocks_high)]
        for case, blocks in cases if middle else []:

            @pl.when(case)
            def _():
                all_of(received, blocks * slots, sem).wait()

        @pl.when(jnp.logical_not(jnp.logical_or(low, high)) if middle else n > 0)
        def _():
            all_of(received, (n - 1) * slots, sem).wait()

    def start_dom(t, way):
        @pl.when(jnp.where(way == 0, dom < n_dom - 1, dom > 0))
        def _():
            dom_copy(t, way).start()

    def start_sub(t):
        for o in range(1, n_sub):
            sub_copy(t, subs[o], sub).start()

    def local_pool(t):
        pools[t][pl.ds(n_fine + sub * hs, hs)] = sub_outs[t][sub]
        base = n_fine + n_sub * hs

        @pl.when(dom == 0)
        def _():
            pools[t][pl.ds(base, hd)] = jnp.zeros((hd, rows, lat), pools[t].dtype)

        @pl.when(dom == n_dom - 1)
        def _():
            pools[t][pl.ds(base + hd, hd)] = jnp.zeros((hd, rows, lat), pools[t].dtype)

    def wait_halo(t):
        all_of(pools[t], (n_sub - 1) * hs, s_recv.at[t]).wait()

        @pl.when(dom > 0)
        def _():
            dom_copy(t, 0).wait_recv()

        @pl.when(dom < n_dom - 1)
        def _():
            dom_copy(t, 1).wait_recv()

    def finish_halo_sends(t):
        all_of(pools[t], (n_sub - 1) * hs, s_send.at[t]).wait()

        @pl.when(dom < n_dom - 1)
        def _():
            dom_copy(t, 0).wait_send()

        @pl.when(dom > 0)
        def _():
            dom_copy(t, 1).wait_send()

    first_way = jnp.where(column == 0, 1, 0)
    ways = [first_way, 1 - first_way]

    with jax.named_scope("A_load"):
        for copy in loads[:3]:
            copy.wait()
        gather_dom(0)
    with jax.named_scope("B_barrier"):
        pl.semaphore_wait(barrier, greeted)

    def tell(about):
        return lambda to: pl.semaphore_signal(
            ready.at[about], inc=1, device_id=(to, sub), device_id_type=MESH
        )

    @pl.when(layer < layers - 1)
    def _():
        tell(layer)(dom + width)

    @pl.when(layer > 0)
    def _():
        tell(layer)(dom - width)

    with jax.named_scope("C_halo"):
        loads[3].wait()
        loads[4].wait()

        @pl.when(jnp.logical_or(low, high))
        def _():
            for copy in relay_copies():
                copy.start()

        for way in ways:
            start_dom(0, way)
        gather_sub(0)
        start_sub(0)
    for copy in loads[5:8]:
        copy.wait()
    for copy in loads[8:]:
        copy.start()
    with jax.named_scope("D_gcoarse"):

        def gather_coarse(d, _):
            for s in range(slots):
                coarse_out[d, s] = coarse[coarse_send[0, s, d]]
            return 0

        lax.fori_loop(0, n, gather_coarse, 0, unroll=4)
        received[pl.ds(me * slots, slots)] = coarse_out[me]

    def send(to_layer, which, copy, skip=False):
        for c in which:
            for s in range(n_sub):
                if c or s or not skip:
                    copy(to_layer * width + columns[c], subs[s]).start()

    def direct(to_layer, which):
        across = jnp.where(to_layer < middle, high, low)

        @pl.when(jnp.logical_not(across))
        def _():
            send(to_layer, which, coarse_copy)

    here, aside = range(1), range(1, width)

    with jax.named_scope("E_ready"):
        for k in range(1, layers):

            @pl.when(layer >= k)
            def _():
                pl.semaphore_wait(ready.at[layer - k], 1)

                @pl.when(layer < layers - 1)
                def _():
                    tell(layer - k)(dom + width)

                direct(layer - k, here)

            @pl.when(layer + k < layers)
            def _():
                pl.semaphore_wait(ready.at[layer + k], 1)

                @pl.when(layer > 0)
                def _():
                    tell(layer + k)(dom - width)

                direct(layer + k, here)

        for k in reversed(range(1, layers)):

            @pl.when(layer >= k)
            def _():
                direct(layer - k, aside)

            @pl.when(layer + k < layers)
            def _():
                direct(layer + k, aside)

        send(layer, here, coarse_copy, True)
        send(layer, aside, coarse_copy)

    half = width * n_sub

    def relay(first, last):
        for copy in relay_copies():
            copy.wait_recv()

        def gather_relay(d, _):
            for s in range(slots):
                relay_out[d, s] = relay_in[relay_send[0, s, d]]
            return 0

        lax.fori_loop(first * half, last * half, gather_relay, 0, unroll=4)
        for which in (here, aside):
            for away in range(1, last - first):
                send(layer + away if first else layer - away, which, passed_on)
            send(layer, which, passed_on, which is here)
        received[pl.ds(mated * slots, slots)] = relay_out[me]

    with jax.named_scope("F_relay"):
        if middle:

            @pl.when(low)
            def _():
                relay(0, middle)

            @pl.when(high)
            def _():
                relay(middle, layers)

    pools[0][pl.ds(0, n_fine)] = held[0][...]
    local_pool(0)

    live = block_count[0]
    chunk = math.gcd(n_fine, 16)

    def matmul(x, w):
        return jnp.dot(x, w, preferred_element_type=jnp.float32)

    def product(weights, table, index, tiles, b):
        picked = jnp.concatenate([table[index[k, b]] for k in range(tiles)], axis=0)
        return matmul(weights[b], picked).astype(jnp.bfloat16)

    def flat(ref, at):
        return ref[at].reshape(-1, lat)

    def second_layer(t):
        wide = w_out[t].astype(jnp.float32)
        wide = wide - jnp.mean(wide, axis=-1, keepdims=True)
        high = wide.astype(jnp.bfloat16)
        low = (wide - high.astype(jnp.float32)).astype(jnp.bfloat16)
        return jnp.concatenate([high, low], axis=1)

    def activate(hidden):
        return jnp.maximum(hidden, 0.0).astype(jnp.bfloat16)

    def centre(hidden, split):
        halves = matmul(hidden, split)
        return halves[:, :lat] + halves[:, lat:]

    def normalize(t, h, centred):
        variance = jnp.mean(centred * centred, axis=-1, keepdims=True)
        normed = centred * lax.rsqrt(variance + 1e-05) * ln_gain[pl.ds(t, 1)]
        return h.astype(jnp.float32) + normed

    def finish(t, h, hidden, split):
        return normalize(t, h, centre(activate(hidden), split))

    def staggered(pieces, stages):
        held_back = {}
        for i in range(len(pieces) + len(stages) - 1):
            for s, stage in enumerate(stages):
                if 0 <= i - s < len(pieces):
                    held_back[i - s] = stage(pieces[i - s], held_back.get(i - s))

    def alive(updated, first):
        shape = (updated.shape[0] // rows, rows, lat)
        block = first + lax.broadcasted_iota(jnp.int32, shape, 0)
        updated = updated.reshape(shape)
        return jnp.where(block < live, updated, 0.0).astype(out.dtype)

    def chunks(body):
        def step(c, _):
            body(c, pl.ds(c * chunk, chunk))
            return 0

        lax.fori_loop(0, n_fine // chunk, step, 0)

    for t in range(steps):
        with jax.named_scope("F_weights"):
            if t == 0:
                for copy in loads[10:]:
                    copy.wait()
            split = second_layer(t)
            w_own = w_in[t, :lat]
            w_sum = w_in[t, lat : 2 * lat]
            w_interp = w_in[t, 2 * lat :]
            w_ends = jnp.concatenate([w_own, w_interp], axis=0)
            bias = b_in[pl.ds(t, 1)]
        if t > 0:
            with jax.named_scope("G_pre"):

                def before(c, at):
                    ends = jnp.concatenate([flat(held[t], at), flat(interp, at)], axis=1)
                    partial[at] = (matmul(ends, w_ends) + bias).reshape(chunk, rows, lat)

                chunks(before)
        with jax.named_scope("H_waithalo"):
            wait_halo(t)
            if t == 0:
                loads[8].wait()
        with jax.named_scope("I_product"):

            size = math.gcd(n_fine, 4 if t == 0 else 4)
            pieces = range(0, n_fine, size)

            def gathered(first, _):
                blocks = range(first, first + size)
                total = [product(adj, pools[t], adj_index, k_a, b) for b in blocks]
                return jnp.concatenate(total, axis=0)

            def started(first, total):
                at = pl.ds(first, size)
                ends = jnp.concatenate([flat(held[t], at), total], axis=1)
                hidden = matmul(ends, w_in[t, : 2 * lat]) + bias
                partial[at] = hidden.reshape(size, rows, lat)

            def activated(first, total):
                at = pl.ds(first, size)
                return activate(flat(partial, at) + matmul(total, w_sum))

            def centred(first, hidden):
                return centre(hidden, split)

            def updated(first, values):
                at = pl.ds(first, size)
                values = alive(normalize(t, flat(held[t], at), values), first)
                if t == steps - 1:
                    out[at] = values
                else:
                    held[t + 1][at] = values

            if t == 0:
                staggered(pieces, [gathered, started])
            else:
                staggered(pieces, [gathered, activated, centred, updated])
        if t == 0:
            with jax.named_scope("J_waitcoarse"):
                loads[9].wait()
                coarse_wait(c_recv, n - 2, n - 2)
            if steps > 1:
                with jax.named_scope("K_early"):
                    def early(picks):
                        mixed = jnp.concatenate(
                            [product(iw, received, interp_slot, k_i, g) for g in picks]
                        )
                        hidden = jnp.concatenate([partial[g] for g in picks])
                        own = jnp.concatenate([held[0][g] for g in picks])
                        updated = finish(0, own, hidden + matmul(mixed, w_interp), split)
                        for i, g in enumerate(picks):
                            one = updated[i * rows : (i + 1) * rows]
                            yield jnp.where(g < live, one, 0.0).astype(out.dtype)

                    for way in ways:
                        picks = [halo_dom_send[0, way, s] for s in range(hd)]
                        for s, one in enumerate(early(picks)):
                            dom_outs[1][way, s] = one
                        start_dom(1, way)
                    places = [(subs[o], s) for o in range(1, n_sub) for s in range(hs)]
                    picks = [halo_sub_send[0, peer, s] for peer, s in places]
                    for (peer, s), one in zip(places, early(picks)):
                        sub_outs[1][peer, s] = one
                    start_sub(1)
            with jax.named_scope("L_update"):

                def interpolated(c, at):
                    for u in range(chunk):
                        b = c * chunk + u
                        interp[b] = product(iw, received, interp_slot, k_i, b)
                    hidden = flat(partial, at) + matmul(flat(interp, at), w_interp)
                    updated = finish(t, flat(held[t], at), hidden, split)
                    updated = alive(updated, c * chunk)
                    if steps == 1:
                        out[at] = updated
                    else:
                        held[1][at] = updated

                chunks(interpolated)
        if t < steps - 1:
            with jax.named_scope("M_send"):
                if t > 0:
                    gather_dom(t + 1)
                    for way in ways:
                        start_dom(t + 1, way)
                if t > 0:
                    gather_sub(t + 1)
                    start_sub(t + 1)
                else:
                    for s in range(hs):
                        sub_outs[1][sub, s] = held[1][halo_sub_send[0, sub, s]]
                pools[t + 1][pl.ds(0, n_fine)] = held[t + 1][...]
                local_pool(t + 1)

    with jax.named_scope("N_finish"):
        for t in range(steps):
            finish_halo_sends(t)
        coarse_wait(c_send, 2 * middle * half - 2, 2 * (layers - middle) * half - 2)

        @pl.when(jnp.logical_or(low, high))
        def _():
            for copy in relay_copies():
                copy.wait_send()


def per_device(
    n_dom,
    n_sub,
    fine_latent,
    coarse_latent,
    adj_index,
    adj_weight,
    interp_slot,
    interp_weight,
    coarse_send,
    halo_sub_send,
    halo_dom_send,
    block_count,
    w_in,
    b_in,
    w_out,
    ln_gain,
):
    n = n_dom * n_sub
    width = max(w for w in range(1, n_dom + 1) if n_dom % w == 0 and w * w <= n_dom)
    steps = w_in.shape[0]
    n_fine, rows, lat = fine_latent.shape
    slots = coarse_send.shape[2]
    hs, hd = halo_sub_send.shape[2], halo_dom_send.shape[2]
    pool = n_fine + n_sub * hs + 2 * hd
    kind = fine_latent.dtype

    def vmem(*lead):
        return pltpu.VMEM(lead + (rows, lat), kind)

    dma = pltpu.SemaphoreType.DMA
    args = (
        fine_latent,
        coarse_latent,
        adj_index.T,
        adj_weight,
        interp_slot.T,
        interp_weight,
        coarse_send.transpose(0, 2, 1),
        halo_sub_send,
        halo_dom_send,
        block_count,
        w_in,
        b_in,
        w_out,
        ln_gain,
    )
    scratch = (
        [vmem(n_fine)] * steps
        + [vmem(pool)] * steps
        + [vmem(n_sub, hs)] * steps
        + [vmem(2, hd)] * steps
        + [
            pltpu.VMEM(coarse_latent.shape, kind),
            pltpu.VMEM(adj_weight.shape, kind),
            pltpu.VMEM(interp_weight.shape, kind),
            vmem(n, slots),
            vmem(n * slots),
            pltpu.VMEM(coarse_latent.shape, kind),
            vmem(n, slots),
            vmem(n_fine),
            pltpu.VMEM((n_fine, rows, lat), jnp.float32),
            pltpu.VMEM(w_in.shape, w_in.dtype),
            pltpu.VMEM(b_in.shape, b_in.dtype),
            pltpu.VMEM(w_out.shape, w_out.dtype),
            pltpu.VMEM(ln_gain.shape, ln_gain.dtype),
        ]
        + [pltpu.SMEM(args[i].shape, jnp.int32) for i in (2, 4, 6, 7, 8, 9, 6)]
        + [
            dma((8,)),
            pltpu.SemaphoreType.REGULAR((n_dom // width,)),
            dma((2,)),
            dma((2,)),
            dma,
            dma,
            dma((steps,)),
            dma((steps,)),
            dma((steps, 2)),
            dma((steps, 2)),
        ]
    )
    hbm = pl.BlockSpec(memory_space=pltpu.HBM)
    return pl.pallas_call(
        functools.partial(kernel, n_dom, n_sub, width, steps),
        out_shape=pltpu.VMEM(fine_latent.shape, kind),
        in_specs=[hbm] * 14,
        scratch_shapes=scratch,
        compiler_params=pltpu.CompilerParams(
            collective_id=0, has_side_effects=True, vmem_limit_bytes=67043328 - fine_latent.size * 2
        ),
        name="graph_steps",
    )(*args)


def solution(mesh):
    placed = (
        P(("dom", "sub"), None, None),
        P(("dom", "sub"), None, None),
        P(("dom", "sub"), None),
        P(("dom", "sub"), None, None),
        P(("dom", "sub"), None),
        P(("dom", "sub"), None, None),
        P(("dom", "sub"), None, None),
        P(("dom", "sub"), None, None),
        P(("dom", "sub"), None, None),
        P(("dom", "sub")),
        P(),
        P(),
        P(),
        P(),
    )
    return jax.shard_map(
        functools.partial(per_device, mesh.shape["dom"], mesh.shape["sub"]),
        mesh=mesh,
        in_specs=placed,
        out_specs=P(("dom", "sub"), None, None),
        check_vma=False,
    )
```

```python
import functools
import math

import jax
import jax.numpy as jnp
from jax import lax
from jax.experimental import pallas as pl
from jax.experimental.pallas import tpu as pltpu
from jax.sharding import PartitionSpec as P

MESH = pl.DeviceIdType.MESH


def kernel(
    n_dom,
    n_sub,
    width,
    steps,
    fine_hbm,
    coarse_hbm,
    adj_index_hbm,
    adj_hbm,
    interp_slot_hbm,
    interp_hbm,
    coarse_send_hbm,
    halo_sub_hbm,
    halo_dom_hbm,
    count_hbm,
    w_in_hbm,
    b_in_hbm,
    w_out_hbm,
    ln_gain_hbm,
    out,
    *scratch,
):
    held = scratch[:steps]
    pools = scratch[steps : 2 * steps]
    sub_outs = scratch[2 * steps : 3 * steps]
    dom_outs = scratch[3 * steps : 4 * steps]
    (
        coarse,
        adj,
        iw,
        coarse_out,
        received,
        relay_in,
        relay_out,
        interp,
        partial,
        w_in,
        b_in,
        w_out,
        ln_gain,
        adj_index,
        interp_slot,
        coarse_send,
        halo_sub_send,
        halo_dom_send,
        block_count,
        relay_send,
        load_sem,
        ready,
        r_send,
        r_recv,
        c_send,
        c_recv,
        s_send,
        s_recv,
        d_send,
        d_recv,
    ) = scratch[4 * steps :]

    n = n_dom * n_sub
    layers = n_dom // width
    middle = layers // 2
    dom, sub = lax.axis_index("dom"), lax.axis_index("sub")
    layer, column = dom // width, dom % width
    me = dom * n_sub + sub
    n_fine, rows, lat = out.shape
    slots = coarse_out.shape[1]
    hs = sub_outs[0].shape[1]
    hd = dom_outs[0].shape[1]
    k_a, k_i = adj_index.shape[0], interp_slot.shape[0]

    barrier = pltpu.get_barrier_semaphore()

    def wrapped(position, size):
        return jnp.where(position >= size, position - size, position)

    subs = [wrapped(sub + o, n_sub) for o in range(n_sub)]
    columns = [wrapped(column + o, width) for o in range(width)]

    def greet(to, other):
        pl.semaphore_signal(barrier, inc=1, device_id=(to, other), device_id_type=MESH)

    edges = [(layer < layers - 1, dom + width), (layer > 0, dom - width)]
    if width > 1:
        edges += [
            (jnp.logical_and(column == width - 1, dom < n_dom - 1), dom + 1),
            (jnp.logical_and(column == 0, dom > 0), dom - 1),
        ]

    for there, to in edges:

        @pl.when(there)
        def _(to=to):
            greet(to, sub)

    for c in range(width):
        for s in range(n_sub):
            if c or s:
                greet(layer * width + columns[c], subs[s])
    greeted = width * n_sub - 1
    for there, _ in edges:
        greeted = greeted + jnp.where(there, 1, 0)

    loads = [
        pltpu.make_async_copy(src, dst, load_sem.at[i % 8])
        for i, (src, dst) in enumerate(
            [
                (fine_hbm, held[0]),
                (halo_dom_hbm, halo_dom_send),
                (halo_sub_hbm, halo_sub_send),
                (coarse_send_hbm, coarse_send),
                (coarse_hbm, coarse),
                (adj_index_hbm, adj_index),
                (interp_slot_hbm, interp_slot),
                (count_hbm, block_count),
                (adj_hbm, adj),
                (interp_hbm, iw),
                (w_in_hbm, w_in),
                (b_in_hbm, b_in),
                (w_out_hbm, w_out),
                (ln_gain_hbm, ln_gain),
            ]
        )
    ]
    for copy in loads[:8]:
        copy.start()

    def gather_sub(t):
        for i in range(n_sub):
            for s in range(hs):
                sub_outs[t][i, s] = held[t][halo_sub_send[0, i, s]]

    def gather_dom(t):
        for i in range(2):
            for s in range(hd):
                dom_outs[t][i, s] = held[t][halo_dom_send[0, i, s]]

    def sub_copy(t, peer, owner):
        return pltpu.make_async_remote_copy(
            src_ref=sub_outs[t].at[peer],
            dst_ref=pools[t].at[pl.ds(n_fine + owner * hs, hs)],
            send_sem=s_send.at[t],
            recv_sem=s_recv.at[t],
            device_id=(dom, peer),
            device_id_type=MESH,
        )

    def dom_copy(t, way):
        target = dom + 1 - 2 * way
        return pltpu.make_async_remote_copy(
            src_ref=dom_outs[t].at[way],
            dst_ref=pools[t].at[pl.ds(n_fine + n_sub * hs + way * hd, hd)],
            send_sem=d_send.at[t, way],
            recv_sem=d_recv.at[t, way],
            device_id=(target, sub),
            device_id_type=MESH,
        )

    def coarse_copy(to, other):
        return pltpu.make_async_remote_copy(
            src_ref=coarse_out.at[to * n_sub + other],
            dst_ref=received.at[pl.ds(me * slots, slots)],
            send_sem=c_send,
            recv_sem=c_recv,
            device_id=(to, other),
            device_id_type=MESH,
        )

    low, high = layer == middle - 1, layer == middle
    mate = jnp.where(low, dom + width, dom - width)
    mated = mate * n_sub + sub

    def relay_copies():
        pairs = [(coarse, relay_in), (coarse_send, relay_send)]
        return [
            pltpu.make_async_remote_copy(
                src_ref=src,
                dst_ref=dst,
                send_sem=r_send.at[i],
                recv_sem=r_recv.at[i],
                device_id=(mate, sub),
                device_id_type=MESH,
            )
            for i, (src, dst) in enumerate(pairs)
        ]

    def passed_on(to, other):
        peer = to * n_sub + other
        return pltpu.make_async_remote_copy(
            src_ref=relay_out.at[peer],
            dst_ref=received.at[pl.ds(mated * slots, slots)],
            send_sem=c_send,
            recv_sem=c_recv,
            device_id=(to, other),
            device_id_type=MESH,
        )

    def all_of(ref, blocks, sem):
        part = ref.at[pl.ds(0, blocks)]
        return pltpu.make_async_copy(part, part, sem)

    def coarse_wait(sem, blocks_low, blocks_high):
        cases = [(low, blocks_low), (high, blocks_high)]
        for case, blocks in cases if middle else []:

            @pl.when(case)
            def _():
                all_of(received, blocks * slots, sem).wait()

        @pl.when(jnp.logical_not(jnp.logical_or(low, high)) if middle else n > 0)
        def _():
            all_of(received, (n - 1) * slots, sem).wait()

    def start_dom(t, way):
        @pl.when(jnp.where(way == 0, dom < n_dom - 1, dom > 0))
        def _():
            dom_copy(t, way).start()

    def start_sub(t):
        for o in range(1, n_sub):
            sub_copy(t, subs[o], sub).start()

    def local_pool(t):
        pools[t][pl.ds(n_fine + sub * hs, hs)] = sub_outs[t][sub]
        base = n_fine + n_sub * hs

        @pl.when(dom == 0)
        def _():
            pools[t][pl.ds(base, hd)] = jnp.zeros((hd, rows, lat), pools[t].dtype)

        @pl.when(dom == n_dom - 1)
        def _():
            pools[t][pl.ds(base + hd, hd)] = jnp.zeros((hd, rows, lat), pools[t].dtype)

    def wait_halo(t):
        all_of(pools[t], (n_sub - 1) * hs, s_recv.at[t]).wait()

        @pl.when(dom > 0)
        def _():
            dom_copy(t, 0).wait_recv()

        @pl.when(dom < n_dom - 1)
        def _():
            dom_copy(t, 1).wait_recv()

    def finish_halo_sends(t):
        all_of(pools[t], (n_sub - 1) * hs, s_send.at[t]).wait()

        @pl.when(dom < n_dom - 1)
        def _():
            dom_copy(t, 0).wait_send()

        @pl.when(dom > 0)
        def _():
            dom_copy(t, 1).wait_send()

    first_way = jnp.where(column == 0, 1, 0)
    ways = [first_way, 1 - first_way]

    with jax.named_scope("A_load"):
        for copy in loads[:3]:
            copy.wait()
        gather_dom(0)
    with jax.named_scope("B_barrier"):
        pl.semaphore_wait(barrier, greeted)

    def tell(about):
        return lambda to: pl.semaphore_signal(
            ready.at[about], inc=1, device_id=(to, sub), device_id_type=MESH
        )

    @pl.when(layer < layers - 1)
    def _():
        tell(layer)(dom + width)

    @pl.when(layer > 0)
    def _():
        tell(layer)(dom - width)

    with jax.named_scope("C_halo"):
        loads[3].wait()
        loads[4].wait()

        @pl.when(jnp.logical_or(low, high))
        def _():
            for copy in relay_copies():
                copy.start()

        for way in ways:
            start_dom(0, way)
        gather_sub(0)
        start_sub(0)
    for copy in loads[5:8]:
        copy.wait()
    for copy in loads[8:]:
        copy.start()
    with jax.named_scope("D_gcoarse"):

        def gather_coarse(d, _):
            for s in range(slots):
                coarse_out[d, s] = coarse[coarse_send[0, s, d]]
            return 0

        lax.fori_loop(0, n, gather_coarse, 0, unroll=4)
        received[pl.ds(me * slots, slots)] = coarse_out[me]

    def send(to_layer, which, copy, skip=False):
        for c in which:
            for s in range(n_sub):
                if c or s or not skip:
                    copy(to_layer * width + columns[c], subs[s]).start()

    def direct(to_layer, which, busy=None):
        across = jnp.where(to_layer < middle, high, low)
        go = jnp.logical_not(across)
        if busy is not None:
            crossing = (to_layer < middle) != (layer < middle)
            last = jnp.where(layer < middle, column == 0, column == width - 1)
            go = jnp.logical_and(go, jnp.logical_and(crossing, last) == busy)

        @pl.when(go)
        def _():
            send(to_layer, which, coarse_copy)

    here, aside = range(1), range(1, width)

    with jax.named_scope("E_ready"):
        for k in range(1, layers):

            @pl.when(layer >= k)
            def _():
                pl.semaphore_wait(ready.at[layer - k], 1)

                @pl.when(layer < layers - 1)
                def _():
                    tell(layer - k)(dom + width)

                direct(layer - k, here, False)

            @pl.when(layer + k < layers)
            def _():
                pl.semaphore_wait(ready.at[layer + k], 1)

                @pl.when(layer > 0)
                def _():
                    tell(layer + k)(dom - width)

                direct(layer + k, here, False)

        for k in reversed(range(1, layers)):

            @pl.when(layer >= k)
            def _():
                direct(layer - k, aside)

            @pl.when(layer + k < layers)
            def _():
                direct(layer + k, aside)

        for k in reversed(range(1, layers)):

            @pl.when(layer >= k)
            def _():
                direct(layer - k, here, True)

            @pl.when(layer + k < layers)
            def _():
                direct(layer + k, here, True)

        send(layer, here, coarse_copy, True)
        send(layer, aside, coarse_copy)

    half = width * n_sub

    def relay(first, last):
        for copy in relay_copies():
            copy.wait_recv()

        def gather_relay(d, _):
            for s in range(slots):
                relay_out[d, s] = relay_in[relay_send[0, s, d]]
            return 0

        lax.fori_loop(first * half, last * half, gather_relay, 0, unroll=4)
        for which in (here, aside):
            for away in range(1, last - first):
                send(layer + away if first else layer - away, which, passed_on)
            send(layer, which, passed_on, which is here)
        received[pl.ds(mated * slots, slots)] = relay_out[me]

    with jax.named_scope("F_relay"):
        if middle:

            @pl.when(low)
            def _():
                relay(0, middle)

            @pl.when(high)
            def _():
                relay(middle, layers)

    pools[0][pl.ds(0, n_fine)] = held[0][...]
    local_pool(0)

    live = block_count[0]
    chunk = math.gcd(n_fine, 16)

    def matmul(x, w):
        return jnp.dot(x, w, preferred_element_type=jnp.float32)

    def product(weights, table, index, tiles, b):
        picked = jnp.concatenate([table[index[k, b]] for k in range(tiles)], axis=0)
        return matmul(weights[b], picked).astype(jnp.bfloat16)

    def flat(ref, at):
        return ref[at].reshape(-1, lat)

    def second_layer(t):
        wide = w_out[t].astype(jnp.float32)
        wide = wide - jnp.mean(wide, axis=-1, keepdims=True)
        high = wide.astype(jnp.bfloat16)
        low = (wide - high.astype(jnp.float32)).astype(jnp.bfloat16)
        return jnp.concatenate([high, low], axis=1)

    def activate(hidden):
        return jnp.maximum(hidden, 0.0).astype(jnp.bfloat16)

    def centre(hidden, split):
        halves = matmul(hidden, split)
        return halves[:, :lat] + halves[:, lat:]

    def normalize(t, h, centred):
        variance = jnp.mean(centred * centred, axis=-1, keepdims=True)
        normed = centred * lax.rsqrt(variance + 1e-05) * ln_gain[pl.ds(t, 1)]
        return h.astype(jnp.float32) + normed

    def finish(t, h, hidden, split):
        return normalize(t, h, centre(activate(hidden), split))

    def staggered(pieces, stages):
        held_back = {}
        for i in range(len(pieces) + len(stages) - 1):
            for s, stage in enumerate(stages):
                if 0 <= i - s < len(pieces):
                    held_back[i - s] = stage(pieces[i - s], held_back.get(i - s))

    def alive(updated, first):
        shape = (updated.shape[0] // rows, rows, lat)
        block = first + lax.broadcasted_iota(jnp.int32, shape, 0)
        updated = updated.reshape(shape)
        return jnp.where(block < live, updated, 0.0).astype(out.dtype)

    def chunks(body):
        def step(c, _):
            body(c, pl.ds(c * chunk, chunk))
            return 0

        lax.fori_loop(0, n_fine // chunk, step, 0)

    for t in range(steps):
        with jax.named_scope("F_weights"):
            if t == 0:
                for copy in loads[10:]:
                    copy.wait()
            split = second_layer(t)
            w_own = w_in[t, :lat]
            w_sum = w_in[t, lat : 2 * lat]
            w_interp = w_in[t, 2 * lat :]
            w_ends = jnp.concatenate([w_own, w_interp], axis=0)
            bias = b_in[pl.ds(t, 1)]
        if t > 0:
            with jax.named_scope("G_pre"):

                def before(c, at):
                    ends = jnp.concatenate([flat(held[t], at), flat(interp, at)], axis=1)
                    partial[at] = (matmul(ends, w_ends) + bias).reshape(chunk, rows, lat)

                chunks(before)
        with jax.named_scope("H_waithalo"):
            wait_halo(t)
            if t == 0:
                loads[8].wait()
        with jax.named_scope("I_product"):

            size = math.gcd(n_fine, 4 if t == 0 else 4)
            pieces = range(0, n_fine, size)

            def gathered(first, _):
                blocks = range(first, first + size)
                total = [product(adj, pools[t], adj_index, k_a, b) for b in blocks]
                return jnp.concatenate(total, axis=0)

            def started(first, total):
                at = pl.ds(first, size)
                ends = jnp.concatenate([flat(held[t], at), total], axis=1)
                hidden = matmul(ends, w_in[t, : 2 * lat]) + bias
                partial[at] = hidden.reshape(size, rows, lat)

            def activated(first, total):
                at = pl.ds(first, size)
                return activate(flat(partial, at) + matmul(total, w_sum))

            def centred(first, hidden):
                return centre(hidden, split)

            def updated(first, values):
                at = pl.ds(first, size)
                values = alive(normalize(t, flat(held[t], at), values), first)
                if t == steps - 1:
                    out[at] = values
                else:
                    held[t + 1][at] = values

            if t == 0:
                staggered(pieces, [gathered, started])
            else:
                staggered(pieces, [gathered, activated, centred, updated])
        if t == 0:
            with jax.named_scope("J_waitcoarse"):
                loads[9].wait()
                coarse_wait(c_recv, n - 2, n - 2)
            if steps > 1:
                with jax.named_scope("K_early"):
                    def early(picks):
                        mixed = jnp.concatenate(
                            [product(iw, received, interp_slot, k_i, g) for g in picks]
                        )
                        hidden = jnp.concatenate([partial[g] for g in picks])
                        own = jnp.concatenate([held[0][g] for g in picks])
                        updated = finish(0, own, hidden + matmul(mixed, w_interp), split)
                        for i, g in enumerate(picks):
                            one = updated[i * rows : (i + 1) * rows]
                            yield jnp.where(g < live, one, 0.0).astype(out.dtype)

                    for way in ways[:1]:
                        picks = [halo_dom_send[0, way, s] for s in range(hd)]
                        for s, one in enumerate(early(picks)):
                            dom_outs[1][way, s] = one
                        start_dom(1, way)
                    places = [(subs[o], s) for o in range(1, n_sub) for s in range(hs)]
                    picks = [halo_sub_send[0, peer, s] for peer, s in places]
                    for (peer, s), one in zip(places, early(picks)):
                        sub_outs[1][peer, s] = one
                    start_sub(1)
                    for way in ways[1:]:
                        picks = [halo_dom_send[0, way, s] for s in range(hd)]
                        for s, one in enumerate(early(picks)):
                            dom_outs[1][way, s] = one
                        start_dom(1, way)
            with jax.named_scope("L_update"):

                def interpolated(c, at):
                    for u in range(chunk):
                        b = c * chunk + u
                        interp[b] = product(iw, received, interp_slot, k_i, b)
                    hidden = flat(partial, at) + matmul(flat(interp, at), w_interp)
                    updated = finish(t, flat(held[t], at), hidden, split)
                    updated = alive(updated, c * chunk)
                    if steps == 1:
                        out[at] = updated
                    else:
                        held[1][at] = updated

                chunks(interpolated)
        if t < steps - 1:
            with jax.named_scope("M_send"):
                if t > 0:
                    gather_dom(t + 1)
                    for way in ways:
                        start_dom(t + 1, way)
                if t > 0:
                    gather_sub(t + 1)
                    start_sub(t + 1)
                else:
                    for s in range(hs):
                        sub_outs[1][sub, s] = held[1][halo_sub_send[0, sub, s]]
                pools[t + 1][pl.ds(0, n_fine)] = held[t + 1][...]
                local_pool(t + 1)

    with jax.named_scope("N_finish"):
        for t in range(steps):
            finish_halo_sends(t)
        coarse_wait(c_send, 2 * middle * half - 2, 2 * (layers - middle) * half - 2)

        @pl.when(jnp.logical_or(low, high))
        def _():
            for copy in relay_copies():
                copy.wait_send()


def per_device(
    n_dom,
    n_sub,
    fine_latent,
    coarse_latent,
    adj_index,
    adj_weight,
    interp_slot,
    interp_weight,
    coarse_send,
    halo_sub_send,
    halo_dom_send,
    block_count,
    w_in,
    b_in,
    w_out,
    ln_gain,
):
    n = n_dom * n_sub
    width = max(w for w in range(1, n_dom + 1) if n_dom % w == 0 and w * w <= n_dom)
    steps = w_in.shape[0]
    n_fine, rows, lat = fine_latent.shape
    slots = coarse_send.shape[2]
    hs, hd = halo_sub_send.shape[2], halo_dom_send.shape[2]
    pool = n_fine + n_sub * hs + 2 * hd
    kind = fine_latent.dtype

    def vmem(*lead):
        return pltpu.VMEM(lead + (rows, lat), kind)

    dma = pltpu.SemaphoreType.DMA
    args = (
        fine_latent,
        coarse_latent,
        adj_index.T,
        adj_weight,
        interp_slot.T,
        interp_weight,
        coarse_send.transpose(0, 2, 1),
        halo_sub_send,
        halo_dom_send,
        block_count,
        w_in,
        b_in,
        w_out,
        ln_gain,
    )
    scratch = (
        [vmem(n_fine)] * steps
        + [vmem(pool)] * steps
        + [vmem(n_sub, hs)] * steps
        + [vmem(2, hd)] * steps
        + [
            pltpu.VMEM(coarse_latent.shape, kind),
            pltpu.VMEM(adj_weight.shape, kind),
            pltpu.VMEM(interp_weight.shape, kind),
            vmem(n, slots),
            vmem(n * slots),
            pltpu.VMEM(coarse_latent.shape, kind),
            vmem(n, slots),
            vmem(n_fine),
            pltpu.VMEM((n_fine, rows, lat), jnp.float32),
            pltpu.VMEM(w_in.shape, w_in.dtype),
            pltpu.VMEM(b_in.shape, b_in.dtype),
            pltpu.VMEM(w_out.shape, w_out.dtype),
            pltpu.VMEM(ln_gain.shape, ln_gain.dtype),
        ]
        + [pltpu.SMEM(args[i].shape, jnp.int32) for i in (2, 4, 6, 7, 8, 9, 6)]
        + [
            dma((8,)),
            pltpu.SemaphoreType.REGULAR((n_dom // width,)),
            dma((2,)),
            dma((2,)),
            dma,
            dma,
            dma((steps,)),
            dma((steps,)),
            dma((steps, 2)),
            dma((steps, 2)),
        ]
    )
    hbm = pl.BlockSpec(memory_space=pltpu.HBM)
    return pl.pallas_call(
        functools.partial(kernel, n_dom, n_sub, width, steps),
        out_shape=pltpu.VMEM(fine_latent.shape, kind),
        in_specs=[hbm] * 14,
        scratch_shapes=scratch,
        compiler_params=pltpu.CompilerParams(
            collective_id=0, has_side_effects=True, vmem_limit_bytes=67043328 - fine_latent.size * 2
        ),
        name="graph_steps",
    )(*args)


def solution(mesh):
    placed = (
        P(("dom", "sub"), None, None),
        P(("dom", "sub"), None, None),
        P(("dom", "sub"), None),
        P(("dom", "sub"), None, None),
        P(("dom", "sub"), None),
        P(("dom", "sub"), None, None),
        P(("dom", "sub"), None, None),
        P(("dom", "sub"), None, None),
        P(("dom", "sub"), None, None),
        P(("dom", "sub")),
        P(),
        P(),
        P(),
        P(),
    )
    return jax.shard_map(
        functools.partial(per_device, mesh.shape["dom"], mesh.shape["sub"]),
        mesh=mesh,
        in_specs=placed,
        out_specs=P(("dom", "sub"), None, None),
        check_vma=False,
    )
```

```python
import functools
import math

import jax
import jax.numpy as jnp
from jax import lax
from jax.experimental import pallas as pl
from jax.experimental.pallas import tpu as pltpu
from jax.sharding import PartitionSpec as P

MESH = pl.DeviceIdType.MESH


def kernel(
    n_dom,
    n_sub,
    width,
    steps,
    fine_hbm,
    coarse_hbm,
    adj_index_hbm,
    adj_hbm,
    interp_slot_hbm,
    interp_hbm,
    coarse_send_hbm,
    halo_sub_hbm,
    halo_dom_hbm,
    count_hbm,
    w_in_hbm,
    b_in_hbm,
    w_out_hbm,
    ln_gain_hbm,
    out,
    *scratch,
):
    held = scratch[:steps]
    pools = scratch[steps : 2 * steps]
    sub_outs = scratch[2 * steps : 3 * steps]
    dom_outs = scratch[3 * steps : 4 * steps]
    (
        coarse,
        adj,
        iw,
        coarse_out,
        received,
        relay_in,
        relay_out,
        interp,
        partial,
        w_in,
        b_in,
        w_out,
        ln_gain,
        adj_index,
        interp_slot,
        coarse_send,
        halo_sub_send,
        halo_dom_send,
        block_count,
        relay_send,
        load_sem,
        ready,
        r_send,
        r_recv,
        c_send,
        c_recv,
        s_send,
        s_recv,
        d_send,
        d_recv,
    ) = scratch[4 * steps :]

    n = n_dom * n_sub
    layers = n_dom // width
    middle = layers // 2
    dom, sub = lax.axis_index("dom"), lax.axis_index("sub")
    layer, column = dom // width, dom % width
    me = dom * n_sub + sub
    n_fine, rows, lat = out.shape
    slots = coarse_out.shape[1]
    hs = sub_outs[0].shape[1]
    hd = dom_outs[0].shape[1]
    k_a, k_i = adj_index.shape[0], interp_slot.shape[0]

    barrier = pltpu.get_barrier_semaphore()

    def wrapped(position, size):
        return jnp.where(position >= size, position - size, position)

    subs = [wrapped(sub + o, n_sub) for o in range(n_sub)]
    columns = [wrapped(column + o, width) for o in range(width)]

    def greet(to, other):
        pl.semaphore_signal(barrier, inc=1, device_id=(to, other), device_id_type=MESH)

    edges = [(layer < layers - 1, dom + width), (layer > 0, dom - width)]
    if width > 1:
        edges += [
            (jnp.logical_and(column == width - 1, dom < n_dom - 1), dom + 1),
            (jnp.logical_and(column == 0, dom > 0), dom - 1),
        ]

    for there, to in edges:

        @pl.when(there)
        def _(to=to):
            greet(to, sub)

    for c in range(width):
        for s in range(n_sub):
            if c or s:
                greet(layer * width + columns[c], subs[s])
    greeted = width * n_sub - 1
    for there, _ in edges:
        greeted = greeted + jnp.where(there, 1, 0)

    loads = [
        pltpu.make_async_copy(src, dst, load_sem.at[i % 8])
        for i, (src, dst) in enumerate(
            [
                (fine_hbm, held[0]),
                (halo_dom_hbm, halo_dom_send),
                (halo_sub_hbm, halo_sub_send),
                (coarse_send_hbm, coarse_send),
                (coarse_hbm, coarse),
                (adj_index_hbm, adj_index),
                (interp_slot_hbm, interp_slot),
                (count_hbm, block_count),
                (adj_hbm, adj),
                (interp_hbm, iw),
                (w_in_hbm, w_in),
                (b_in_hbm, b_in),
                (w_out_hbm, w_out),
                (ln_gain_hbm, ln_gain),
            ]
        )
    ]
    for copy in loads[:8]:
        copy.start()

    def gather_sub(t):
        for i in range(n_sub):
            for s in range(hs):
                sub_outs[t][i, s] = held[t][halo_sub_send[0, i, s]]

    def gather_dom(t):
        for i in range(2):
            for s in range(hd):
                dom_outs[t][i, s] = held[t][halo_dom_send[0, i, s]]

    def sub_copy(t, peer, owner):
        return pltpu.make_async_remote_copy(
            src_ref=sub_outs[t].at[peer],
            dst_ref=pools[t].at[pl.ds(n_fine + owner * hs, hs)],
            send_sem=s_send.at[t],
            recv_sem=s_recv.at[t],
            device_id=(dom, peer),
            device_id_type=MESH,
        )

    def dom_copy(t, way):
        target = dom + 1 - 2 * way
        return pltpu.make_async_remote_copy(
            src_ref=dom_outs[t].at[way],
            dst_ref=pools[t].at[pl.ds(n_fine + n_sub * hs + way * hd, hd)],
            send_sem=d_send.at[t, way],
            recv_sem=d_recv.at[t, way],
            device_id=(target, sub),
            device_id_type=MESH,
        )

    def coarse_copy(to, other):
        return pltpu.make_async_remote_copy(
            src_ref=coarse_out.at[to * n_sub + other],
            dst_ref=received.at[pl.ds(me * slots, slots)],
            send_sem=c_send,
            recv_sem=c_recv,
            device_id=(to, other),
            device_id_type=MESH,
        )

    low, high = layer == middle - 1, layer == middle
    mate = jnp.where(low, dom + width, dom - width)
    mated = mate * n_sub + sub

    def relay_copies():
        pairs = [(coarse, relay_in), (coarse_send, relay_send)]
        return [
            pltpu.make_async_remote_copy(
                src_ref=src,
                dst_ref=dst,
                send_sem=r_send.at[i],
                recv_sem=r_recv.at[i],
                device_id=(mate, sub),
                device_id_type=MESH,
            )
            for i, (src, dst) in enumerate(pairs)
        ]

    def passed_on(to, other):
        peer = to * n_sub + other
        return pltpu.make_async_remote_copy(
            src_ref=relay_out.at[peer],
            dst_ref=received.at[pl.ds(mated * slots, slots)],
            send_sem=c_send,
            recv_sem=c_recv,
            device_id=(to, other),
            device_id_type=MESH,
        )

    def all_of(ref, blocks, sem):
        part = ref.at[pl.ds(0, blocks)]
        return pltpu.make_async_copy(part, part, sem)

    def coarse_wait(sem, blocks_low, blocks_high):
        cases = [(low, blocks_low), (high, blocks_high)]
        for case, blocks in cases if middle else []:

            @pl.when(case)
            def _():
                all_of(received, blocks * slots, sem).wait()

        @pl.when(jnp.logical_not(jnp.logical_or(low, high)) if middle else n > 0)
        def _():
            all_of(received, (n - 1) * slots, sem).wait()

    def start_dom(t, way):
        @pl.when(jnp.where(way == 0, dom < n_dom - 1, dom > 0))
        def _():
            dom_copy(t, way).start()

    def start_sub(t):
        for o in range(1, n_sub):
            sub_copy(t, subs[o], sub).start()

    def local_pool(t):
        pools[t][pl.ds(n_fine + sub * hs, hs)] = sub_outs[t][sub]
        base = n_fine + n_sub * hs

        @pl.when(dom == 0)
        def _():
            pools[t][pl.ds(base, hd)] = jnp.zeros((hd, rows, lat), pools[t].dtype)

        @pl.when(dom == n_dom - 1)
        def _():
            pools[t][pl.ds(base + hd, hd)] = jnp.zeros((hd, rows, lat), pools[t].dtype)

    def wait_halo(t):
        all_of(pools[t], (n_sub - 1) * hs, s_recv.at[t]).wait()

        @pl.when(dom > 0)
        def _():
            dom_copy(t, 0).wait_recv()

        @pl.when(dom < n_dom - 1)
        def _():
            dom_copy(t, 1).wait_recv()

    def finish_halo_sends(t):
        all_of(pools[t], (n_sub - 1) * hs, s_send.at[t]).wait()

        @pl.when(dom < n_dom - 1)
        def _():
            dom_copy(t, 0).wait_send()

        @pl.when(dom > 0)
        def _():
            dom_copy(t, 1).wait_send()

    first_way = jnp.where(column == 0, 1, 0)
    ways = [first_way, 1 - first_way]

    with jax.named_scope("A_load"):
        for copy in loads[:3]:
            copy.wait()
        gather_dom(0)
    with jax.named_scope("B_barrier"):
        pl.semaphore_wait(barrier, greeted)

    def tell(about):
        return lambda to: pl.semaphore_signal(
            ready.at[about], inc=1, device_id=(to, sub), device_id_type=MESH
        )

    @pl.when(layer < layers - 1)
    def _():
        tell(layer)(dom + width)

    @pl.when(layer > 0)
    def _():
        tell(layer)(dom - width)

    with jax.named_scope("C_halo"):
        loads[3].wait()
        loads[4].wait()

        @pl.when(jnp.logical_or(low, high))
        def _():
            for copy in relay_copies():
                copy.start()

        for way in ways:
            start_dom(0, way)
        gather_sub(0)
        start_sub(0)
    for copy in loads[5:8]:
        copy.wait()
    for copy in loads[8:]:
        copy.start()
    with jax.named_scope("D_gcoarse"):

        def gather_coarse(d, _):
            for s in range(slots):
                coarse_out[d, s] = coarse[coarse_send[0, s, d]]
            return 0

        lax.fori_loop(0, n, gather_coarse, 0, unroll=4)
        received[pl.ds(me * slots, slots)] = coarse_out[me]

    def send(to_layer, which, copy, skip=False):
        for c in which:
            for s in range(n_sub):
                if c or s or not skip:
                    copy(to_layer * width + columns[c], subs[s]).start()

    def direct(to_layer, which, busy=None):
        across = jnp.where(to_layer < middle, high, low)
        go = jnp.logical_not(across)
        if busy is not None:
            crossing = (to_layer < middle) != (layer < middle)
            last = jnp.where(layer < middle, column == 0, column == width - 1)
            go = jnp.logical_and(go, jnp.logical_and(crossing, last) == busy)

        @pl.when(go)
        def _():
            send(to_layer, which, coarse_copy)

    here, aside = range(1), range(1, width)

    with jax.named_scope("E_ready"):
        send(layer, here, coarse_copy, True)
        send(layer, aside, coarse_copy)
        for k in range(1, layers):

            @pl.when(layer >= k)
            def _():
                pl.semaphore_wait(ready.at[layer - k], 1)

                @pl.when(layer < layers - 1)
                def _():
                    tell(layer - k)(dom + width)

                direct(layer - k, here, False)

            @pl.when(layer + k < layers)
            def _():
                pl.semaphore_wait(ready.at[layer + k], 1)

                @pl.when(layer > 0)
                def _():
                    tell(layer + k)(dom - width)

                direct(layer + k, here, False)

        for k in reversed(range(1, layers)):

            @pl.when(layer >= k)
            def _():
                direct(layer - k, aside)

            @pl.when(layer + k < layers)
            def _():
                direct(layer + k, aside)

        for k in reversed(range(1, layers)):

            @pl.when(layer >= k)
            def _():
                direct(layer - k, here, True)

            @pl.when(layer + k < layers)
            def _():
                direct(layer + k, here, True)


    half = width * n_sub

    def relay(first, last):
        for copy in relay_copies():
            copy.wait_recv()

        def gather_relay(d, _):
            for s in range(slots):
                relay_out[d, s] = relay_in[relay_send[0, s, d]]
            return 0

        lax.fori_loop(first * half, last * half, gather_relay, 0, unroll=4)
        for which in (here, aside):
            for away in range(1, last - first):
                send(layer + away if first else layer - away, which, passed_on)
            send(layer, which, passed_on, which is here)
        received[pl.ds(mated * slots, slots)] = relay_out[me]

    with jax.named_scope("F_relay"):
        if middle:

            @pl.when(low)
            def _():
                relay(0, middle)

            @pl.when(high)
            def _():
                relay(middle, layers)

    pools[0][pl.ds(0, n_fine)] = held[0][...]
    local_pool(0)

    live = block_count[0]
    chunk = math.gcd(n_fine, 16)

    def matmul(x, w):
        return jnp.dot(x, w, preferred_element_type=jnp.float32)

    def product(weights, table, index, tiles, b):
        picked = jnp.concatenate([table[index[k, b]] for k in range(tiles)], axis=0)
        return matmul(weights[b], picked).astype(jnp.bfloat16)

    def flat(ref, at):
        return ref[at].reshape(-1, lat)

    def second_layer(t):
        wide = w_out[t].astype(jnp.float32)
        wide = wide - jnp.mean(wide, axis=-1, keepdims=True)
        high = wide.astype(jnp.bfloat16)
        low = (wide - high.astype(jnp.float32)).astype(jnp.bfloat16)
        return jnp.concatenate([high, low], axis=1)

    def activate(hidden):
        return jnp.maximum(hidden, 0.0).astype(jnp.bfloat16)

    def centre(hidden, split):
        halves = matmul(hidden, split)
        return halves[:, :lat] + halves[:, lat:]

    def normalize(t, h, centred):
        variance = jnp.mean(centred * centred, axis=-1, keepdims=True)
        normed = centred * lax.rsqrt(variance + 1e-05) * ln_gain[pl.ds(t, 1)]
        return h.astype(jnp.float32) + normed

    def finish(t, h, hidden, split):
        return normalize(t, h, centre(activate(hidden), split))

    def staggered(pieces, stages):
        held_back = {}
        for i in range(len(pieces) + len(stages) - 1):
            for s, stage in enumerate(stages):
                if 0 <= i - s < len(pieces):
                    held_back[i - s] = stage(pieces[i - s], held_back.get(i - s))

    def alive(updated, first):
        shape = (updated.shape[0] // rows, rows, lat)
        block = first + lax.broadcasted_iota(jnp.int32, shape, 0)
        updated = updated.reshape(shape)
        return jnp.where(block < live, updated, 0.0).astype(out.dtype)

    def chunks(body):
        def step(c, _):
            body(c, pl.ds(c * chunk, chunk))
            return 0

        lax.fori_loop(0, n_fine // chunk, step, 0)

    for t in range(steps):
        with jax.named_scope("F_weights"):
            if t == 0:
                for copy in loads[10:]:
                    copy.wait()
            split = second_layer(t)
            w_own = w_in[t, :lat]
            w_sum = w_in[t, lat : 2 * lat]
            w_interp = w_in[t, 2 * lat :]
            w_ends = jnp.concatenate([w_own, w_interp], axis=0)
            bias = b_in[pl.ds(t, 1)]
        if t > 0:
            with jax.named_scope("G_pre"):

                def before(c, at):
                    ends = jnp.concatenate([flat(held[t], at), flat(interp, at)], axis=1)
                    partial[at] = (matmul(ends, w_ends) + bias).reshape(chunk, rows, lat)

                chunks(before)
        with jax.named_scope("H_waithalo"):
            wait_halo(t)
            if t == 0:
                loads[8].wait()
        with jax.named_scope("I_product"):

            size = math.gcd(n_fine, 4 if t == 0 else 4)
            pieces = range(0, n_fine, size)

            def gathered(first, _):
                blocks = range(first, first + size)
                total = [product(adj, pools[t], adj_index, k_a, b) for b in blocks]
                return jnp.concatenate(total, axis=0)

            def started(first, total):
                at = pl.ds(first, size)
                ends = jnp.concatenate([flat(held[t], at), total], axis=1)
                hidden = matmul(ends, w_in[t, : 2 * lat]) + bias
                partial[at] = hidden.reshape(size, rows, lat)

            def activated(first, total):
                at = pl.ds(first, size)
                return activate(flat(partial, at) + matmul(total, w_sum))

            def centred(first, hidden):
                return centre(hidden, split)

            def updated(first, values):
                at = pl.ds(first, size)
                values = alive(normalize(t, flat(held[t], at), values), first)
                if t == steps - 1:
                    out[at] = values
                else:
                    held[t + 1][at] = values

            if t == 0:
                staggered(pieces, [gathered, started])
            else:
                staggered(pieces, [gathered, activated, centred, updated])
        if t == 0:
            with jax.named_scope("J_waitcoarse"):
                loads[9].wait()
                coarse_wait(c_recv, n - 2, n - 2)
            if steps > 1:
                with jax.named_scope("K_early"):
                    def early(picks):
                        mixed = jnp.concatenate(
                            [product(iw, received, interp_slot, k_i, g) for g in picks]
                        )
                        hidden = jnp.concatenate([partial[g] for g in picks])
                        own = jnp.concatenate([held[0][g] for g in picks])
                        updated = finish(0, own, hidden + matmul(mixed, w_interp), split)
                        for i, g in enumerate(picks):
                            one = updated[i * rows : (i + 1) * rows]
                            yield jnp.where(g < live, one, 0.0).astype(out.dtype)

                    for way in ways[:1]:
                        picks = [halo_dom_send[0, way, s] for s in range(hd)]
                        for s, one in enumerate(early(picks)):
                            dom_outs[1][way, s] = one
                        start_dom(1, way)
                    places = [(subs[o], s) for o in range(1, n_sub) for s in range(hs)]
                    picks = [halo_sub_send[0, peer, s] for peer, s in places]
                    for (peer, s), one in zip(places, early(picks)):
                        sub_outs[1][peer, s] = one
                    start_sub(1)
                    for way in ways[1:]:
                        picks = [halo_dom_send[0, way, s] for s in range(hd)]
                        for s, one in enumerate(early(picks)):
                            dom_outs[1][way, s] = one
                        start_dom(1, way)
            with jax.named_scope("L_update"):

                def interpolated(c, at):
                    for u in range(chunk):
                        b = c * chunk + u
                        interp[b] = product(iw, received, interp_slot, k_i, b)
                    hidden = flat(partial, at) + matmul(flat(interp, at), w_interp)
                    updated = finish(t, flat(held[t], at), hidden, split)
                    updated = alive(updated, c * chunk)
                    if steps == 1:
                        out[at] = updated
                    else:
                        held[1][at] = updated

                chunks(interpolated)
        if t < steps - 1:
            with jax.named_scope("M_send"):
                if t > 0:
                    gather_dom(t + 1)
                    for way in ways:
                        start_dom(t + 1, way)
                if t > 0:
                    gather_sub(t + 1)
                    start_sub(t + 1)
                else:
                    for s in range(hs):
                        sub_outs[1][sub, s] = held[1][halo_sub_send[0, sub, s]]
                pools[t + 1][pl.ds(0, n_fine)] = held[t + 1][...]
                local_pool(t + 1)

    with jax.named_scope("N_finish"):
        for t in range(steps):
            finish_halo_sends(t)
        coarse_wait(c_send, 2 * middle * half - 2, 2 * (layers - middle) * half - 2)

        @pl.when(jnp.logical_or(low, high))
        def _():
            for copy in relay_copies():
                copy.wait_send()


def per_device(
    n_dom,
    n_sub,
    fine_latent,
    coarse_latent,
    adj_index,
    adj_weight,
    interp_slot,
    interp_weight,
    coarse_send,
    halo_sub_send,
    halo_dom_send,
    block_count,
    w_in,
    b_in,
    w_out,
    ln_gain,
):
    n = n_dom * n_sub
    width = max(w for w in range(1, n_dom + 1) if n_dom % w == 0 and w * w <= n_dom)
    steps = w_in.shape[0]
    n_fine, rows, lat = fine_latent.shape
    slots = coarse_send.shape[2]
    hs, hd = halo_sub_send.shape[2], halo_dom_send.shape[2]
    pool = n_fine + n_sub * hs + 2 * hd
    kind = fine_latent.dtype

    def vmem(*lead):
        return pltpu.VMEM(lead + (rows, lat), kind)

    dma = pltpu.SemaphoreType.DMA
    args = (
        fine_latent,
        coarse_latent,
        adj_index.T,
        adj_weight,
        interp_slot.T,
        interp_weight,
        coarse_send.transpose(0, 2, 1),
        halo_sub_send,
        halo_dom_send,
        block_count,
        w_in,
        b_in,
        w_out,
        ln_gain,
    )
    scratch = (
        [vmem(n_fine)] * steps
        + [vmem(pool)] * steps
        + [vmem(n_sub, hs)] * steps
        + [vmem(2, hd)] * steps
        + [
            pltpu.VMEM(coarse_latent.shape, kind),
            pltpu.VMEM(adj_weight.shape, kind),
            pltpu.VMEM(interp_weight.shape, kind),
            vmem(n, slots),
            vmem(n * slots),
            pltpu.VMEM(coarse_latent.shape, kind),
            vmem(n, slots),
            vmem(n_fine),
            pltpu.VMEM((n_fine, rows, lat), jnp.float32),
            pltpu.VMEM(w_in.shape, w_in.dtype),
            pltpu.VMEM(b_in.shape, b_in.dtype),
            pltpu.VMEM(w_out.shape, w_out.dtype),
            pltpu.VMEM(ln_gain.shape, ln_gain.dtype),
        ]
        + [pltpu.SMEM(args[i].shape, jnp.int32) for i in (2, 4, 6, 7, 8, 9, 6)]
        + [
            dma((8,)),
            pltpu.SemaphoreType.REGULAR((n_dom // width,)),
            dma((2,)),
            dma((2,)),
            dma,
            dma,
            dma((steps,)),
            dma((steps,)),
            dma((steps, 2)),
            dma((steps, 2)),
        ]
    )
    hbm = pl.BlockSpec(memory_space=pltpu.HBM)
    return pl.pallas_call(
        functools.partial(kernel, n_dom, n_sub, width, steps),
        out_shape=pltpu.VMEM(fine_latent.shape, kind),
        in_specs=[hbm] * 14,
        scratch_shapes=scratch,
        compiler_params=pltpu.CompilerParams(
            collective_id=0, has_side_effects=True, vmem_limit_bytes=67043328 - fine_latent.size * 2
        ),
        name="graph_steps",
    )(*args)


def solution(mesh):
    placed = (
        P(("dom", "sub"), None, None),
        P(("dom", "sub"), None, None),
        P(("dom", "sub"), None),
        P(("dom", "sub"), None, None),
        P(("dom", "sub"), None),
        P(("dom", "sub"), None, None),
        P(("dom", "sub"), None, None),
        P(("dom", "sub"), None, None),
        P(("dom", "sub"), None, None),
        P(("dom", "sub")),
        P(),
        P(),
        P(),
        P(),
    )
    return jax.shard_map(
        functools.partial(per_device, mesh.shape["dom"], mesh.shape["sub"]),
        mesh=mesh,
        in_specs=placed,
        out_specs=P(("dom", "sub"), None, None),
        check_vma=False,
    )
```
